128 devices in a mesh: dp: 32 (over y, x, core), expert: 4 (over z).
Axes of the slice: x: 4, y: 4, z: 4, core: 2. Of those that a mesh axis runs over, the one named last changes fastest.
Arguments:
- tokens: bfloat16 [8192, 1024], P(('dp', 'expert')), may hold values from -6 to 6
- expert_ids: int32 [8192, 2], P(('dp', 'expert')), may hold values from 0 to 7, all different within a row; in each aligned block of 64 rows (0 to 63, 64 to 127, ...) at most 20 rows name the same one
- gate_weights: float32 [8192, 2], P(('dp', 'expert')), may hold values from 0.2 to 1
- w_gate: bfloat16 [8, 1024, 4096], P('expert', None, 'dp'), may hold values from -0.1875 to 0.1875
- w_up: bfloat16 [8, 1024, 4096], P('expert', None, 'dp'), may hold values from -0.1875 to 0.1875
- w_down: bfloat16 [8, 4096, 1024], P('expert', 'dp'), may hold values from -0.09375 to 0.09375
- cotangent: bfloat16 [8192, 1024], P(('dp', 'expert')), may hold values from -6 to 6
Outputs:
- mixed: bfloat16 [8192, 1024], P(('dp', 'expert'))
- grad_tokens: bfloat16 [8192, 1024], P(('dp', 'expert'))
- grad_gate: bfloat16 [8, 1024, 4096], P('expert', None, 'dp')
- grad_up: bfloat16 [8, 1024, 4096], P('expert', None, 'dp')
- grad_down: bfloat16 [8, 4096, 1024], P('expert', 'dp')
The draws below stay inside these ranges and needn't reach their ends.
Inputs may be any that keep to these rules, and one draw needn't show every extreme that they name: `expert_ids`: in every aligned block of 64 rows (the rows of one device) no expert is named more than 20 times, a bound that some block reaches; the 2 experts of a row differ.
All inputs are finite; a program needn't handle non-finite values.
Results may differ from the reference program's by a relative error of at most 0.019.
Values may be sent and summed in bfloat16 or wider, within the bound.
A program may use at most 192 MiB of HBM per device.

```python
import math
import jax
import jax.numpy as jnp
import numpy as np
from jax import lax

D = 1024
FF = 4096
EXPERTS = 8
TOP = 2
TOK_DEV = 64
CAP = 20
TOKENS = 8192
N_DP = 32


def steps_of(key, dims, split, smallest, top_value):
    level, own = 1.0, jax.random.fold_in(key, 6)
    for dim, blocks in split:
        heights = jnp.exp(jax.random.uniform(jax.random.fold_in(own, dim), (blocks,), jnp.float32, smallest / len(split), top_value / len(split)))
        level = level * jnp.repeat(heights, dims[dim] // blocks).reshape([-1 if axis == dim else 1 for axis in range(len(dims))])
    return level


def deal_out(own_key, own, number, rows, number_of, top, most, slope):
    sequence = jax.random.permutation(own_key, number_of)
    crowded, common = portions_of(number_of, rows * top, most, slope, True), portions_of(number_of, rows * top, most, slope, False)
    places = jnp.arange(number_of)

    def named(tallies, offset_by):
        used = int((tallies > 0).sum())
        fixed = max(1, used // 4)
        shifted = fixed + (places - fixed + offset_by * (used - fixed)) % max(1, number_of - fixed)
        return jnp.zeros((number_of,), jnp.int32).at[sequence[jnp.where(places < fixed, places, shifted)]].set(jnp.asarray(tallies, jnp.int32))

    tallies = jnp.where(number % 4 == 0, named(crowded, number // 4), named(common, number - number // 4 - 1))
    mixed = jax.random.permutation(jax.random.fold_in(own, 3), number_of)
    donor, taker = mixed[0:number_of // 2 * 2:2], mixed[1:number_of // 2 * 2:2]
    margin = jnp.minimum(tallies[donor] - 1, most - tallies[taker]) // 2
    margin = jnp.where((donor == sequence[0]) | (taker == sequence[0]) | (tallies[taker] == 0), 0, jnp.maximum(margin, 0))
    shifted = jax.random.randint(jax.random.fold_in(own, 4), (number_of // 2,), 0, 1 << 20) % (margin + 1)
    tallies = tallies.at[donor].add(-shifted).at[taker].add(shifted)
    labels = jnp.searchsorted(jnp.cumsum(tallies), jnp.arange(rows * top), side="right").astype(jnp.int32)
    table = labels.reshape(top, rows).T
    table = table[jax.random.permutation(jax.random.fold_in(own, 1), rows)]
    offset_by = jax.random.randint(jax.random.fold_in(own, 2), (rows, 1), 0, top)
    return jnp.take_along_axis(table, (jnp.arange(top)[None, :] + offset_by) % top, axis=1)


def portions_of(count, total, bound, lean, full):
    weights = [(1 << 20) // math.isqrt(standing ** lean) + 1 for standing in range(1, count + 1)]
    largest = bound if full else min(bound, max(-(-total // count), total * weights[0] // sum(weights)))
    least = 1 if total - largest >= count - 1 else 0
    counts, surplus = [largest] + [least] * (count - 1), total - largest - least * (count - 1)
    while surplus > 0:
        free = [i for i in range(1, count) if counts[i] < largest] or [i for i in range(1, count) if counts[i] < bound]
        mass, left = sum([weights[i] for i in free]), surplus
        for i in free:
            addition = min(bound - counts[i], max(1, left * weights[i] // mass), surplus)
            counts[i] = counts[i] + addition
            surplus = surplus - addition
    return np.array(counts)


def bell_draw(own_key, shape, deviation, reach, pieces=(), held_as=jnp.bfloat16):
    array = jax.random.normal(own_key, shape, jnp.float32) * deviation
    if len(pieces) > 0:
        array = steps_of(own_key, shape, pieces, -0.22, 0.18) * array
    return jnp.clip(array, min=-reach, max=reach).astype(held_as)


def setup_inputs(seed: int = 0) -> dict:
    keys = jax.random.split(jax.random.key(seed), 8)
    tokens = bell_draw(keys[0], (TOKENS, D), 1.0, 6.0, ((0, 128),))
    expert_ids_keys = jax.random.split(jax.random.fold_in(keys[1], 1), TOKENS // TOK_DEV)
    expert_ids_turns = jax.random.permutation(jax.random.fold_in(keys[1], 3), TOKENS // TOK_DEV)
    expert_ids = jax.vmap(lambda own, number: deal_out(jax.random.fold_in(keys[1], 2), own, number, TOK_DEV, EXPERTS, TOP, CAP, 2))(expert_ids_keys, expert_ids_turns).reshape((TOKENS, TOP))
    gate_weights = jnp.clip(0.2 + 0.8 * jax.random.uniform(keys[2], (TOKENS, TOP), jnp.float32) ** steps_of(keys[2], (TOKENS, TOP), ((0, 128),), -0.2, 0.2), 0.2, 1.0)
    w_gate = bell_draw(keys[3], (EXPERTS, D, FF), D ** -0.5, 0.1875, ((0, 4), (2, 32)))
    w_up = bell_draw(keys[4], (EXPERTS, D, FF), D ** -0.5, 0.1875, ((0, 4), (2, 32)))
    w_down = bell_draw(keys[5], (EXPERTS, FF, D), FF ** -0.5, 0.09375, ((0, 4), (1, 32)))
    cotangent = bell_draw(keys[6], (TOKENS, D), 1.0, 6.0, ((0, 128),))
    return dict(tokens=tokens, expert_ids=expert_ids, gate_weights=gate_weights, w_gate=w_gate, w_up=w_up, w_down=w_down, cotangent=cotangent)


def round_groups(parts):
    rounded = lax.optimization_barrier(parts.astype(jnp.bfloat16))
    return jnp.sum(rounded.astype(jnp.float32), axis=0).astype(jnp.bfloat16)


def expert_pass(operands):
    x_rows, dy_rows, wg, wu, wd = operands
    fpart = FF // N_DP
    count = x_rows.shape[0]
    gate = jnp.dot(x_rows, wg, preferred_element_type=jnp.float32)
    up = jnp.dot(x_rows, wu, preferred_element_type=jnp.float32)
    sig = jax.nn.sigmoid(gate)
    act = gate * sig
    hidden = (act * up).astype(jnp.bfloat16)
    hid_split = hidden.astype(jnp.float32).reshape(count, N_DP, fpart)
    parts = jnp.einsum("rpf,pfd->prd", hid_split, wd.astype(jnp.float32).reshape(N_DP, fpart, D))
    expert_out = round_groups(parts)
    dact = jnp.dot(dy_rows, wd.T, preferred_element_type=jnp.float32)
    grad_hg = (dact * up * sig * (1.0 + gate * (1.0 - sig))).astype(jnp.bfloat16)
    grad_hu = (dact * act).astype(jnp.bfloat16)
    grad_wd = jnp.dot(hidden.T, dy_rows, preferred_element_type=jnp.float32).astype(jnp.bfloat16)
    grad_wg = jnp.dot(x_rows.T, grad_hg, preferred_element_type=jnp.float32).astype(jnp.bfloat16)
    grad_wu = jnp.dot(x_rows.T, grad_hu, preferred_element_type=jnp.float32).astype(jnp.bfloat16)
    back_parts = jnp.einsum("rpf,dpf->prd", grad_hg.astype(jnp.float32).reshape(count, N_DP, fpart),
                            wg.astype(jnp.float32).reshape(D, N_DP, fpart))
    back_parts = back_parts + jnp.einsum("rpf,dpf->prd", grad_hu.astype(jnp.float32).reshape(count, N_DP, fpart),
                                         wu.astype(jnp.float32).reshape(D, N_DP, fpart))
    token_part = round_groups(back_parts)
    return expert_out, token_part, grad_wg, grad_wu, grad_wd


def reference(tokens, expert_ids, gate_weights, w_gate, w_up, w_down, cotangent):
    blocks = TOKENS // TOK_DEV
    flat = expert_ids.reshape(blocks, TOK_DEV * TOP)
    onehot = (flat[:, :, None] == jnp.arange(EXPERTS, dtype=jnp.int32)[None, None, :]).astype(jnp.int32)
    before = jnp.sum((jnp.cumsum(onehot, axis=1) - onehot) * onehot, axis=2)
    column = jnp.arange(blocks, dtype=jnp.int32)[:, None] * CAP + before
    eflat = flat.reshape(-1).astype(jnp.int32)
    cflat = column.reshape(-1).astype(jnp.int32)
    rows_x = jnp.repeat(tokens, TOP, axis=0)
    buf_x = jnp.zeros((EXPERTS, blocks * CAP, D), jnp.bfloat16).at[eflat, cflat].set(rows_x)
    rows_d = (gate_weights[:, :, None] * cotangent[:, None, :].astype(jnp.float32)).reshape(TOKENS * TOP, D)
    buf_d = jnp.zeros((EXPERTS, blocks * CAP, D), jnp.bfloat16).at[eflat, cflat].set(rows_d.astype(jnp.bfloat16))
    expert_out, token_part, grad_gate, grad_up, grad_down = lax.map(expert_pass, (buf_x, buf_d, w_gate, w_up, w_down))
    picked = expert_out[eflat, cflat].astype(jnp.float32).reshape(TOKENS, TOP, D)
    mixed = jnp.sum(gate_weights[:, :, None] * picked, axis=1).astype(jnp.bfloat16)
    back = token_part[eflat, cflat].astype(jnp.float32).reshape(TOKENS, TOP, D)
    grad_tokens = jnp.sum(back, axis=1).astype(jnp.bfloat16)
    return mixed, grad_tokens, grad_gate, grad_up, grad_down
```

```python
import jax
import jax.numpy as jnp
from jax import lax
from jax.sharding import PartitionSpec as P


def body(tokens, expert_ids, gate_weights, w_gate, w_up, w_down, cotangent):
    owners = lax.axis_size("expert")
    n_dp = lax.axis_size("dp")
    tok_count, width = tokens.shape
    top_count = expert_ids.shape[1]
    exp_local = w_gate.shape[0]
    experts_all = exp_local * owners
    capacity = max(2, 5 * tok_count * top_count // (4 * experts_all))
    same_core = [list(range(c, n_dp, 2)) for c in range(2)]
    swap = [(i, i ^ 1) for i in range(n_dp)]

    flat = expert_ids.reshape(-1)
    onehot = (flat[:, None] == jnp.arange(experts_all, dtype=jnp.int32)[None, :]).astype(jnp.int32)
    before = jnp.sum((jnp.cumsum(onehot, axis=0) - onehot) * onehot, axis=1)
    slot = flat * capacity + before
    placer = (jnp.arange(experts_all * capacity, dtype=jnp.int32)[:, None] == slot[None, :]).astype(
        jnp.bfloat16
    )

    def place(rows):
        buffer = jnp.dot(placer, rows, preferred_element_type=jnp.float32).astype(jnp.bfloat16)
        return buffer.reshape(owners, exp_local, capacity, width)

    def spread(buffer):
        arrived = lax.all_to_all(buffer, "expert", split_axis=0, concat_axis=0, tiled=True)
        arrived = arrived.transpose(1, 0, 2, 3).reshape(exp_local, owners * capacity, width)
        return lax.all_gather(arrived, "dp", axis=0, tiled=False, axis_index_groups=same_core)

    def collect(partial):
        summed = lax.psum_scatter(
            partial, "dp", scatter_dimension=0, tiled=False, axis_index_groups=same_core
        )
        summed = summed.reshape(exp_local, owners, capacity, width).transpose(1, 0, 2, 3)
        return lax.all_to_all(summed, "expert", split_axis=0, concat_axis=0, tiled=True)

    def unpack(results):
        flat_out = results.reshape(experts_all * capacity, width)
        picked = lax.dot_general(
            placer, flat_out, (((0,), (0,)), ((), ())), preferred_element_type=jnp.float32
        )
        return picked.reshape(tok_count, top_count, width)

    def other(v):
        return lax.ppermute(v, "dp", swap)

    wg2, wu2, wd2 = other(w_gate), other(w_up), other(w_down)
    wg = jnp.concatenate([w_gate, wg2], axis=2)
    wu = jnp.concatenate([w_up, wu2], axis=2)
    wd = jnp.concatenate([w_down, wd2], axis=1)
    half = w_gate.shape[2]

    buf_x = place(jnp.repeat(tokens, top_count, axis=0))
    rows_d = (gate_weights[:, :, None] * cotangent[:, None, :].astype(jnp.float32)).reshape(
        tok_count * top_count, width
    )
    buf_d = place(rows_d.astype(jnp.bfloat16))
    xs = spread(buf_x)
    gate = jnp.einsum("pjcd,jdf->pjcf", xs, wg, preferred_element_type=jnp.float32)
    up = jnp.einsum("pjcd,jdf->pjcf", xs, wu, preferred_element_type=jnp.float32)
    sig = jax.nn.sigmoid(gate)
    act = gate * sig
    hidden = (act * up).astype(jnp.bfloat16)
    part_o = jnp.einsum("pjcf,jfd->pjcd", hidden, wd, preferred_element_type=jnp.float32)
    out_rows = collect(part_o.astype(jnp.bfloat16))
    mixed = jnp.sum(gate_weights[:, :, None] * unpack(out_rows), axis=1).astype(jnp.bfloat16)

    ds = spread(buf_d)
    dact = jnp.einsum("pjcd,jfd->pjcf", ds, wd, preferred_element_type=jnp.float32)
    dg = (dact * up * sig * (1.0 + gate * (1.0 - sig))).astype(jnp.bfloat16)
    du = (dact * act).astype(jnp.bfloat16)
    part_v = jnp.einsum("pjcf,jdf->pjcd", dg, wg, preferred_element_type=jnp.float32)
    part_v = part_v + jnp.einsum("pjcf,jdf->pjcd", du, wu, preferred_element_type=jnp.float32)
    grad_tokens = jnp.sum(unpack(collect(part_v.astype(jnp.bfloat16))), axis=1).astype(jnp.bfloat16)

    gd = jnp.einsum("pjcf,pjcd->jfd", hidden, ds, preferred_element_type=jnp.float32)
    gg = jnp.einsum("pjcd,pjcf->jdf", xs, dg, preferred_element_type=jnp.float32)
    gu = jnp.einsum("pjcd,pjcf->jdf", xs, du, preferred_element_type=jnp.float32)

    def total(mine, theirs):
        arrived = other(theirs.astype(jnp.bfloat16))
        return (mine + arrived.astype(jnp.float32)).astype(jnp.bfloat16)

    grad_down = total(gd[:, :half], gd[:, half:])
    grad_gate = total(gg[:, :, :half], gg[:, :, half:])
    grad_up = total(gu[:, :, :half], gu[:, :, half:])
    return (mixed, grad_tokens, grad_gate, grad_up, grad_down)


def solution(mesh):
    rows = P(("dp", "expert"), None)
    cols = P("expert", None, "dp")
    down = P("expert", "dp", None)
    return jax.shard_map(
        body,
        mesh=mesh,
        in_specs=(rows, rows, rows, cols, cols, down, rows),
        out_specs=(rows, rows, cols, cols, down),
        check_vma=False,
    )
```

```python
import jax
import jax.numpy as jnp
from jax import lax
from jax.experimental import pallas as pl
from jax.experimental.pallas import tpu as pltpu
from jax.sharding import PartitionSpec as P

MESH = pl.DeviceIdType.MESH
BF, F32 = jnp.bfloat16, jnp.float32
TOK, D, CAP = 64, 1024, 20
PLANES, EXP = 4, 2
SLAB = 48
ALL = PLANES * SLAB
ROWS = PLANES * CAP
SLOTS = 8
MINE = SLOTS * ROWS
HALF = D // 2
FP = 128
HID = 4 * FP
COPIES = 128


def dot(a, b, contract=(1, 0)):
    return lax.dot_general(a, b, (((contract[0],), (contract[1],)), ((), ())), preferred_element_type=F32)


class Net:
    def __init__(self, send, recv):
        self.send, self.recv, self.all = send, recv, []

    def go(self, src, dst, device):
        k = len(self.all)
        copy = pltpu.make_async_remote_copy(
            src_ref=src, dst_ref=dst, send_sem=self.send.at[k], recv_sem=self.recv.at[k],
            device_id=device, device_id_type=MESH,
        )
        copy.start()
        self.all.append(copy)
        return copy


def got(*copies):
    for copy in copies:
        copy.wait_recv()


def left(ref, e, s):
    return ref.at[e, s, :, pl.ds(0, HALF)]


def right(ref, e, s):
    return ref.at[e, s, :, pl.ds(HALF, HALF)]


class Gather:
    def __init__(self, net, ref, xp, yu, yd):
        self.net, self.ref, self.xp, self.yu, self.yd = net, ref, xp, yu, yd

    def start(self):
        go, g = self.net.go, self.ref
        self.x0 = go(g.at[0, 0], g.at[0, 4], self.xp)
        self.u1 = go(g.at[1, 0], g.at[1, 3], self.yu)
        self.d1 = go(g.at[1, 0], g.at[1, 1], self.yd)
        self.u00 = go(g.at[0, 0], g.at[0, 3], self.yu)
        self.d00 = go(g.at[0, 0], g.at[0, 1], self.yd)
        self.x1 = [go(g.at[1, 0], g.at[1, 4], self.xp)]

    def step2(self):
        go, g = self.net.go, self.ref
        got(self.x0)
        self.u01 = go(g.at[0, 4], g.at[0, 7], self.yu)
        self.d01 = go(g.at[0, 4], g.at[0, 5], self.yd)
        got(self.u1)
        self.fu1 = go(left(g, 1, 3), left(g, 1, 2), self.yu)
        self.x1.append(go(g.at[1, 3], g.at[1, 7], self.xp))
        got(self.d1)
        self.fd1 = go(right(g, 1, 1), right(g, 1, 2), self.yd)
        self.x1.append(go(g.at[1, 1], g.at[1, 5], self.xp))
        got(self.u00)
        self.fu00 = go(left(g, 0, 3), left(g, 0, 2), self.yu)
        got(self.d00)
        self.fd00 = go(right(g, 0, 1), right(g, 0, 2), self.yd)

    def step3(self):
        go, g = self.net.go, self.ref
        got(self.u01)
        self.fu01 = go(left(g, 0, 7), left(g, 0, 6), self.yu)
        got(self.d01)
        self.fd01 = go(right(g, 0, 5), right(g, 0, 6), self.yd)
        got(self.fu1, self.fd1)
        self.x1.append(go(g.at[1, 2], g.at[1, 6], self.xp))

    def finish(self, e):
        if e == 0:
            got(self.fu00, self.fd00, self.fu01, self.fd01)
        else:
            got(*self.x1)


def add_half(p, e, s, lo, arrived):
    cols = pl.ds(lo, HALF)
    p[e, s, :, cols] = (p[e, s, :, cols].astype(F32) + arrived[...].astype(F32)).astype(BF)


class Reduce:
    def __init__(self, net, part, near, far, across, xp, yu, yd):
        self.net, self.p, self.near, self.far, self.across = net, part, near, far, across
        self.xp, self.yu, self.yd = xp, yu, yd
        self.ring = {}

    def outer(self, key, e, b):
        go, p = self.net.go, self.p
        self.ring[key] = [
            go(left(p, e, b + 2), self.near.at[key, 0], self.yu),
            go(right(p, e, b + 2), self.near.at[key, 1], self.yd),
        ]

    def free_up(self, key, e, b):
        self.ring[key].append(self.net.go(right(self.p, e, b + 1), right(self.far, key, 0), self.yu))

    def free_down(self, key, e, b):
        self.ring[key].append(self.net.go(left(self.p, e, b + 3), left(self.far, key, 1), self.yd))

    def inner(self, key, e, b):
        go, p = self.net.go, self.p
        got(self.ring[key][0])
        add_half(p, e, b + 1, 0, self.near.at[key, 0])
        up = go(left(p, e, b + 1), left(self.far, key, 0), self.yu)
        got(self.ring[key][1])
        add_half(p, e, b + 3, HALF, self.near.at[key, 1])
        down = go(right(p, e, b + 3), right(self.far, key, 1), self.yd)
        self.ring[key] += [up, down]

    def total(self, key, e, b):
        got(*self.ring[key][2:])
        return self.p[e, b].astype(F32) + self.far[key, 0].astype(F32) + self.far[key, 1].astype(F32)

    def start0(self):
        for dx in (1, 0):
            self.outer(dx, 0, 4 * dx)
        for dx in (1, 0):
            self.free_up(dx, 0, 4 * dx)
            self.free_down(dx, 0, 4 * dx)

    def start1(self):
        self.x1 = {dy: self.net.go(self.p.at[1, 4 + dy], self.across.at[dy], self.xp) for dy in (2, 1, 3, 0)}

    def joined(self, dy):
        got(self.x1[dy])
        self.p[1, dy] = (self.p[1, dy].astype(F32) + self.across[dy].astype(F32)).astype(BF)

    def step2(self):
        self.joined(2)
        self.outer(2, 1, 0)
        self.inner(1, 0, 4)
        self.inner(0, 0, 0)
        self.joined(1)
        self.free_up(2, 1, 0)
        self.joined(3)
        self.free_down(2, 1, 0)
        self.joined(0)

    def step3(self):
        self.p[0, 4] = self.total(1, 0, 4).astype(BF)
        self.x0 = self.net.go(self.p.at[0, 4], self.across.at[4], self.xp)
        self.inner(2, 1, 0)

    def step4(self):
        rows0 = self.total(0, 0, 0)
        got(self.x0)
        rows0 = (rows0 + self.across[4].astype(F32)).astype(BF)
        rows1 = self.total(2, 1, 0).astype(BF)
        return jnp.concatenate([rows0, rows1], axis=0)


def kernel(
    tok, ids, gw, cot, wg, wu, wd,
    mixed, gtok, ggate, gup, gdown,
    send_x, send_d, arr_x, arr_d, send_o, send_v, arr_o, arr_v,
    xg, dg, po, pv, near_o, far_o, across_o, near_v, far_v, across_v,
    wgu, wdn, fac_a, fac_b, hid, dgu, pd, pgu, rd, rgu, rd2, rgu2,
    send, recv, local,
):
    dp, z = lax.axis_index("dp"), lax.axis_index("expert")
    core, x, y = dp % 2, (dp // 2) % 4, dp // 8

    def at(yy, xx, cc):
        return ((yy * 4 + xx) * 2 + cc, z)

    xp = at(y, x + 1 - 2 * (x % 2), core)
    xc = at(y, 3 - x, core)
    yu, yd = at((y + 1) % 4, x, core), at((y + 3) % 4, x, core)
    cp = at(y, x, 1 - core)
    zs = {r: (dp, (z + r) % 4) for r in (1, 2, 3)}

    barrier = pltpu.get_barrier_semaphore()
    for device in (xp, xc, yu, yd, cp, zs[1], zs[2], zs[3]):
        pl.semaphore_signal(barrier, inc=1, device_id=device, device_id_type=MESH)

    own = [
        pltpu.make_async_copy(wg, wgu.at[:, :, pl.ds(0, FP)], local.at[0]),
        pltpu.make_async_copy(wu, wgu.at[:, :, pl.ds(HID, FP)], local.at[1]),
        pltpu.make_async_copy(wd, wdn.at[:, pl.ds(0, FP), :], local.at[2]),
    ]
    for copy in own:
        copy.start()

    lane = lax.broadcasted_iota(jnp.int32, (TOK, 128), 1)
    hot = [jnp.where(lane == ids[:, k : k + 1], 1.0, 0.0) for k in range(2)]
    ordered = jnp.where(
        lax.broadcasted_iota(jnp.int32, (TOK, TOK), 1) < lax.broadcasted_iota(jnp.int32, (TOK, TOK), 0), 1.0, 0.0
    )
    before = dot(ordered.astype(BF), (hot[0] + hot[1]).astype(BF))
    col = lax.broadcasted_iota(jnp.int32, (TOK, ALL), 1).astype(F32)
    picks = []
    for k in range(2):
        e = ids[:, k : k + 1]
        plane = lax.shift_right_logical(e, 1)
        rel = plane - z
        rel = jnp.where(rel < 0, rel + PLANES, rel)
        base = rel * SLAB + (e - 2 * plane) * CAP
        place = jnp.sum(hot[k] * before, axis=1, keepdims=True)
        picks.append(jnp.where(col == base.astype(F32) + place, 1.0, 0.0).astype(BF))

    def from_slab(c):
        s = (c >= SLAB).astype(jnp.int32) + (c >= 2 * SLAB).astype(jnp.int32) + (c >= 3 * SLAB).astype(jnp.int32)
        rest = c - SLAB * s
        j = (rest >= CAP).astype(jnp.int32)
        row = j * ROWS + s * CAP + rest - CAP * j
        return jnp.where(rest < EXP * CAP, row, -1)

    into = jnp.where(
        from_slab(lax.broadcasted_iota(jnp.int32, (EXP * ROWS, ALL), 1))
        == lax.broadcasted_iota(jnp.int32, (EXP * ROWS, ALL), 0), 1.0, 0.0,
    ).astype(BF)
    back = jnp.where(
        from_slab(lax.broadcasted_iota(jnp.int32, (ALL, EXP * ROWS), 0))
        == lax.broadcasted_iota(jnp.int32, (ALL, EXP * ROWS), 1), 1.0, 0.0,
    ).astype(BF)

    net = Net(send, recv)
    pl.semaphore_wait(barrier, 8)
    go = net.go

    def slabs_out(rows, send_ref, arr_ref):
        for r in range(PLANES):
            part = rows[r * SLAB : (r + 1) * SLAB].astype(BF)
            if r == 0:
                arr_ref[0] = part
            else:
                send_ref[r] = part
        return [go(send_ref.at[r], arr_ref.at[PLANES - r], zs[r]) for r in (2, 1, 3)]

    slab_rows = dot((picks[0] + picks[1]), tok[...], (0, 0))
    zx = slabs_out(slab_rows, send_x, arr_x)

    def weight(k, lo):
        return wgu.at[:, :, pl.ds(lo + k * FP, FP)]

    def down(k):
        return wdn.at[:, pl.ds(k * FP, FP), :]

    cross = [go(wg, weight(1, 0), xc), go(wu, weight(1, HID), xc), go(wd, down(1), xc)]
    side = [go(wg, weight(2, 0), cp), go(wu, weight(2, HID), cp), go(wd, down(2), cp)]

    cotf = cot[...].astype(F32)
    rows_d = [(gw[:, k : k + 1] * cotf).astype(BF) for k in range(2)]
    zd = slabs_out(dot(picks[0], rows_d[0], (0, 0)) + dot(picks[1], rows_d[1], (0, 0)), send_d, arr_d)

    def chunk_in(arr_ref, g):
        rows = dot(into, arr_ref[...].reshape(ALL, D)).astype(BF)
        g[0, 0] = rows[:ROWS]
        g[1, 0] = rows[ROWS:]

    gx, gd = Gather(net, xg, xp, yu, yd), Gather(net, dg, xp, yu, yd)
    got(*zx)
    chunk_in(arr_x, xg)
    gx.start()
    got(*zd)
    chunk_in(arr_d, dg)
    gx.step2()
    gd.start()
    got(cross[0])
    side.append(go(weight(1, 0), weight(3, 0), cp))
    gx.step3()
    got(cross[1])
    side.append(go(weight(1, HID), weight(3, HID), cp))
    for copy in own:
        copy.wait()
    got(*side)

    def forward(e):
        def tile(n, _):
            cols = pl.ds(pl.multiple_of(n * 256, 256), 256)
            rows = xg[e].reshape(MINE, D)
            gate = dot(rows, wgu[e, :, cols])
            up = dot(rows, wgu[e, :, pl.ds(pl.multiple_of(n * 256 + HID, 256), 256)])
            sig = 1.0 / (1.0 + jnp.exp(-gate))
            act = gate * sig
            hid[e, :, cols] = (act * up).astype(BF)
            fac_b[e, :, cols] = act
            fac_a[e, :, cols] = up * sig * (1.0 + gate * (1.0 - sig))
            return 0

        lax.fori_loop(0, HID // 256, tile, 0)

    def project(e):
        def tile(n, _):
            cols = pl.ds(pl.multiple_of(n * 256, 256), 256)
            po[e, :, :, cols] = dot(hid[e], wdn[e, :, cols]).astype(BF).reshape(SLOTS, ROWS, 256)
            return 0

        lax.fori_loop(0, D // 256, tile, 0)

    gx.finish(0)
    forward(0)
    gd.step2()
    gx.finish(1)
    forward(1)
    gd.step3()
    got(cross[2])
    late = go(down(1), down(3), cp)
    got(late)
    ro = Reduce(net, po, near_o, far_o, across_o, xp, yu, yd)
    rv = Reduce(net, pv, near_v, far_v, across_v, xp, yu, yd)
    project(0)
    ro.start0()
    project(1)
    ro.start1()

    def backward(e):
        def tile(n, _):
            cols = pl.ds(pl.multiple_of(n * 256, 256), 256)
            dact = dot(dg[e].reshape(MINE, D), wdn[e, cols, :], (1, 1))
            dgu[e, :, cols] = (dact * fac_a[e, :, cols]).astype(BF)
            dgu[e, :, pl.ds(pl.multiple_of(n * 256 + HID, 256), 256)] = (dact * fac_b[e, :, cols]).astype(BF)
            return 0

        lax.fori_loop(0, HID // 256, tile, 0)

    def propagate(e):
        def tile(n, _):
            cols = pl.ds(pl.multiple_of(n * 256, 256), 256)
            part = dot(dgu[e], wgu[e, cols, :], (1, 1))
            pv[e, :, :, cols] = part.astype(BF).reshape(SLOTS, ROWS, 256)
            return 0

        lax.fori_loop(0, D // 256, tile, 0)

    def down_grad(e):
        def tile(n, _):
            cols = pl.ds(pl.multiple_of(n * 256, 256), 256)
            pd[e, cols, :] = dot(hid[e, :, cols], dg[e].reshape(MINE, D), (0, 0)).astype(BF)
            return 0

        lax.fori_loop(0, HID // 256, tile, 0)

    def up_grad(e):
        def tile(n, _):
            cols = pl.ds(pl.multiple_of(n * 256, 256), 256)
            pgu[e, cols, :] = dot(xg[e, :, :, cols].reshape(MINE, 256), dgu[e], (0, 0)).astype(BF)
            return 0

        lax.fori_loop(0, D // 256, tile, 0)

    gd.finish(0)
    backward(0)
    gd.finish(1)
    backward(1)
    ro.step2()
    propagate(0)
    rv.start0()
    propagate(1)
    rv.start1()
    ro.step3()
    for e in range(EXP):
        down_grad(e)

    pair = 2 * FP
    share_d = go(pd.at[:, pl.ds(pair, pair), :], rd, cp)
    rv.step2()
    for e in range(EXP):
        up_grad(e)
    share_g = go(pgu.at[:, :, pl.ds(pair, pair)], rgu.at[0], cp)
    share_u = go(pgu.at[:, :, pl.ds(HID + pair, pair)], rgu.at[1], cp)
    got(share_d)
    pd[:, pl.ds(0, pair), :] = (pd[:, pl.ds(0, pair), :].astype(F32) + rd[...].astype(F32)).astype(BF)
    far_d = go(pd.at[:, pl.ds(FP, FP), :], rd2, xc)
    far_g = []
    for i, share in ((0, share_g), (1, share_u)):
        got(share)
        cols = pl.ds(i * HID, pair)

        def add(e, _, i=i, cols=cols):
            pgu[e, :, cols] = (pgu[e, :, cols].astype(F32) + rgu[i, e].astype(F32)).astype(BF)
            return 0

        lax.fori_loop(0, EXP, add, 0)
        far_g.append(go(pgu.at[:, :, pl.ds(i * HID + FP, FP)], rgu2.at[i], xc))
    rv.step3()

    def results_back(rows, send_ref, arr_ref):
        return slabs_out(dot(back, rows), send_ref, arr_ref)

    zo = results_back(ro.step4(), send_o, arr_o)
    zv = results_back(rv.step4(), send_v, arr_v)
    got(*zo)
    rows = arr_o[...].reshape(ALL, D)
    mixed[...] = (gw[:, 0:1] * dot(picks[0], rows) + gw[:, 1:2] * dot(picks[1], rows)).astype(BF)
    got(*zv)
    gtok[...] = dot(picks[0] + picks[1], arr_v[...].reshape(ALL, D)).astype(BF)
    got(far_d)
    gdown[...] = (pd[:, pl.ds(0, FP), :].astype(F32) + rd2[...].astype(F32)).astype(BF)
    for i, out in ((0, ggate), (1, gup)):
        got(far_g[i])
        out[...] = (pgu[:, :, pl.ds(i * HID, FP)].astype(F32) + rgu2[i].astype(F32)).astype(BF)
    for copy in net.all:
        copy.wait_send()


def body(tokens, expert_ids, gate_weights, w_gate, w_up, w_down, cotangent):
    vmem, hbm = pl.BlockSpec(memory_space=pltpu.VMEM), pl.BlockSpec(memory_space=pl.ANY)

    def buf(*shape, dtype=BF):
        return pltpu.VMEM(shape, dtype)

    slab = [buf(PLANES, SLAB, D) for _ in range(8)]
    big = [buf(EXP, SLOTS, ROWS, D) for _ in range(4)]
    rings = [buf(3, 2, ROWS, HALF), buf(3, 2, ROWS, D), buf(5, ROWS, D)] * 2
    scratch = slab + big + rings + [
        buf(EXP, D, 2 * HID), buf(EXP, HID, D),
        buf(EXP, MINE, HID, dtype=F32), buf(EXP, MINE, HID, dtype=F32),
        buf(EXP, MINE, HID), buf(EXP, MINE, 2 * HID),
        buf(EXP, HID, D), buf(EXP, D, 2 * HID),
        buf(EXP, 2 * FP, D), buf(2, EXP, D, 2 * FP), buf(EXP, FP, D), buf(2, EXP, D, FP),
        pltpu.SemaphoreType.DMA((COPIES,)), pltpu.SemaphoreType.DMA((COPIES,)), pltpu.SemaphoreType.DMA((3,)),
    ]
    return pl.pallas_call(
        kernel,
        out_shape=tuple(
            jax.ShapeDtypeStruct(a.shape, BF) for a in (tokens, tokens, w_gate, w_up, w_down)
        ),
        in_specs=[vmem] * 4 + [hbm] * 3,
        out_specs=(vmem,) * 5,
        scratch_shapes=scratch,
        compiler_params=pltpu.CompilerParams(
            collective_id=0, has_side_effects=True, vmem_limit_bytes=67043328
        ),
    )(tokens, expert_ids, gate_weights, cotangent, w_gate, w_up, w_down)


def solution(mesh):
    rows = P(("dp", "expert"), None)
    cols = P("expert", None, "dp")
    down = P("expert", "dp", None)
    return jax.shard_map(
        body,
        mesh=mesh,
        in_specs=(rows, rows, rows, cols, cols, down, rows),
        out_specs=(rows, rows, cols, cols, down),
        check_vma=False,
    )
```

```python
import jax
import jax.numpy as jnp
from jax import lax
from jax.experimental import pallas as pl
from jax.experimental.pallas import tpu as pltpu
from jax.sharding import PartitionSpec as P

MESH = pl.DeviceIdType.MESH
BF, F32 = jnp.bfloat16, jnp.float32
TOK, D, CAP = 64, 1024, 20
PLANES, EXP = 4, 2
SLAB = 48
ALL = PLANES * SLAB
ROWS = PLANES * CAP
SLOTS = 8
MINE = SLOTS * ROWS
HALF = D // 2
FP = 128
HID = 4 * FP
COPIES = 128


def dot(a, b, contract=(1, 0)):
    return lax.dot_general(a, b, (((contract[0],), (contract[1],)), ((), ())), preferred_element_type=F32)


class Net:
    def __init__(self, send, recv):
        self.send, self.recv, self.all = send, recv, []

    def go(self, src, dst, device):
        k = len(self.all)
        copy = pltpu.make_async_remote_copy(
            src_ref=src, dst_ref=dst, send_sem=self.send.at[k], recv_sem=self.recv.at[k],
            device_id=device, device_id_type=MESH,
        )
        copy.start()
        self.all.append(copy)
        return copy


def got(*copies):
    for copy in copies:
        copy.wait_recv()


def left(ref, e, s):
    return ref.at[e, s, :, pl.ds(0, HALF)]


def right(ref, e, s):
    return ref.at[e, s, :, pl.ds(HALF, HALF)]


class Gather:
    def __init__(self, net, ref, xp, yu, yd):
        self.net, self.ref, self.xp, self.yu, self.yd = net, ref, xp, yu, yd

    def start(self):
        go, g = self.net.go, self.ref
        self.x0 = go(g.at[0, 0], g.at[0, 4], self.xp)
        self.u1 = go(g.at[1, 0], g.at[1, 3], self.yu)
        self.d1 = go(g.at[1, 0], g.at[1, 1], self.yd)
        self.u00 = go(g.at[0, 0], g.at[0, 3], self.yu)
        self.d00 = go(g.at[0, 0], g.at[0, 1], self.yd)
        self.x1 = [go(g.at[1, 0], g.at[1, 4], self.xp)]

    def step2(self):
        go, g = self.net.go, self.ref
        got(self.x0)
        self.u01 = go(g.at[0, 4], g.at[0, 7], self.yu)
        self.d01 = go(g.at[0, 4], g.at[0, 5], self.yd)
        got(self.u1)
        self.fu1 = go(left(g, 1, 3), left(g, 1, 2), self.yu)
        self.x1.append(go(g.at[1, 3], g.at[1, 7], self.xp))
        got(self.d1)
        self.fd1 = go(right(g, 1, 1), right(g, 1, 2), self.yd)
        self.x1.append(go(g.at[1, 1], g.at[1, 5], self.xp))
        got(self.u00)
        self.fu00 = go(left(g, 0, 3), left(g, 0, 2), self.yu)
        got(self.d00)
        self.fd00 = go(right(g, 0, 1), right(g, 0, 2), self.yd)

    def step3(self):
        go, g = self.net.go, self.ref
        got(self.u01)
        self.fu01 = go(left(g, 0, 7), left(g, 0, 6), self.yu)
        got(self.d01)
        self.fd01 = go(right(g, 0, 5), right(g, 0, 6), self.yd)
        got(self.fu1, self.fd1)
        self.x1.append(go(g.at[1, 2], g.at[1, 6], self.xp))

    def finish(self, e):
        if e == 0:
            got(self.fu00, self.fd00, self.fu01, self.fd01)
        else:
            got(*self.x1)


def add_half(p, e, s, lo, arrived):
    cols = pl.ds(lo, HALF)
    p[e, s, :, cols] = (p[e, s, :, cols].astype(F32) + arrived[...].astype(F32)).astype(BF)


class Reduce:
    def __init__(self, net, part, near, far, across, xp, yu, yd):
        self.net, self.p, self.near, self.far, self.across = net, part, near, far, across
        self.xp, self.yu, self.yd = xp, yu, yd
        self.ring = {}

    def outer(self, key, e, b):
        go, p = self.net.go, self.p
        self.ring[key] = [
            go(left(p, e, b + 2), self.near.at[key, 0], self.yu),
            go(right(p, e, b + 2), self.near.at[key, 1], self.yd),
        ]

    def free_up(self, key, e, b):
        self.ring[key].append(self.net.go(right(self.p, e, b + 1), right(self.far, key, 0), self.yu))

    def free_down(self, key, e, b):
        self.ring[key].append(self.net.go(left(self.p, e, b + 3), left(self.far, key, 1), self.yd))

    def inner(self, key, e, b):
        go, p = self.net.go, self.p
        got(self.ring[key][0])
        add_half(p, e, b + 1, 0, self.near.at[key, 0])
        up = go(left(p, e, b + 1), left(self.far, key, 0), self.yu)
        got(self.ring[key][1])
        add_half(p, e, b + 3, HALF, self.near.at[key, 1])
        down = go(right(p, e, b + 3), right(self.far, key, 1), self.yd)
        self.ring[key] += [up, down]

    def total(self, key, e, b):
        got(*self.ring[key][2:])
        return self.p[e, b].astype(F32) + self.far[key, 0].astype(F32) + self.far[key, 1].astype(F32)

    def start0(self):
        for dx in (1, 0):
            self.outer(dx, 0, 4 * dx)
        for dx in (1, 0):
            self.free_up(dx, 0, 4 * dx)
            self.free_down(dx, 0, 4 * dx)

    def start1(self):
        self.x1 = {dy: self.net.go(self.p.at[1, 4 + dy], self.across.at[dy], self.xp) for dy in (2, 1, 3, 0)}

    def joined(self, dy):
        got(self.x1[dy])
        self.p[1, dy] = (self.p[1, dy].astype(F32) + self.across[dy].astype(F32)).astype(BF)

    def step2(self):
        self.joined(2)
        self.outer(2, 1, 0)
        self.inner(1, 0, 4)
        self.inner(0, 0, 0)
        self.joined(1)
        self.free_up(2, 1, 0)
        self.joined(3)
        self.free_down(2, 1, 0)
        self.joined(0)

    def step3(self):
        self.p[0, 4] = self.total(1, 0, 4).astype(BF)
        self.x0 = self.net.go(self.p.at[0, 4], self.across.at[4], self.xp)
        self.inner(2, 1, 0)

    def step4(self):
        rows0 = self.total(0, 0, 0)
        got(self.x0)
        rows0 = (rows0 + self.across[4].astype(F32)).astype(BF)
        rows1 = self.total(2, 1, 0).astype(BF)
        return jnp.concatenate([rows0, rows1], axis=0)


def kernel(
    tok, ids, gw, cot, wg, wu, wd,
    pick, arr_o, arr_v, sum_d, sum_gu, far_d, far_gu,
    send_x, send_d, send_o, send_v, arr_x, arr_d, via,
    xg, dg, po, pv, near_o, far_o, across_o, near_v, far_v, across_v,
    wgu, wdn, fac_a, fac_b, hid, dgu, pd, pgu, rd, rgu,
    send, recv, local,
):
    dp, z = lax.axis_index("dp"), lax.axis_index("expert")
    core, x, y = dp % 2, (dp // 2) % 4, dp // 8

    def at(yy, xx, cc):
        return ((yy * 4 + xx) * 2 + cc, z)

    xp = at(y, x + 1 - 2 * (x % 2), core)
    xc = at(y, 3 - x, core)
    yu, yd = at((y + 1) % 4, x, core), at((y + 3) % 4, x, core)
    cp = at(y, x, 1 - core)
    zs = {r: (dp, (z + r) % 4) for r in (1, 2, 3)}

    barrier = pltpu.get_barrier_semaphore()
    for device in (xp, xc, yu, yd, cp, zs[1], zs[2], zs[3]):
        pl.semaphore_signal(barrier, inc=1, device_id=device, device_id_type=MESH)

    own = [
        pltpu.make_async_copy(wg, wgu.at[:, :, pl.ds(0, FP)], local.at[0]),
        pltpu.make_async_copy(wu, wgu.at[:, :, pl.ds(HID, FP)], local.at[1]),
        pltpu.make_async_copy(wd, wdn.at[:, pl.ds(0, FP), :], local.at[2]),
    ]
    for copy in own:
        copy.start()

    expert = lax.broadcasted_iota(jnp.int32, (2 * PLANES, TOK), 0)
    hot = [jnp.where(expert == ids[k : k + 1, :], 1.0, 0.0) for k in range(2)]
    row_t = lax.broadcasted_iota(jnp.int32, (TOK, TOK), 0)
    col_t = lax.broadcasted_iota(jnp.int32, (TOK, TOK), 1)
    before = dot((hot[0] + hot[1]).astype(BF), jnp.where(row_t < col_t, 1.0, 0.0).astype(BF))
    slab_row = lax.broadcasted_iota(jnp.int32, (ALL, TOK), 0).astype(F32)
    picks = []
    for k in range(2):
        e = ids[k : k + 1, :]
        plane = lax.shift_right_logical(e, 1)
        rel = plane - z
        rel = jnp.where(rel < 0, rel + PLANES, rel)
        base = rel * SLAB + (e - 2 * plane) * CAP
        place = jnp.sum(hot[k] * before, axis=0, keepdims=True)
        picks.append(jnp.where(slab_row == base.astype(F32) + place, 1.0, 0.0).astype(BF))
        pick[k] = picks[k]

    def from_slab(c):
        s = (c >= SLAB).astype(jnp.int32) + (c >= 2 * SLAB).astype(jnp.int32) + (c >= 3 * SLAB).astype(jnp.int32)
        rest = c - SLAB * s
        j = (rest >= CAP).astype(jnp.int32)
        row = j * ROWS + s * CAP + rest - CAP * j
        return jnp.where(rest < EXP * CAP, row, -1)

    into = jnp.where(
        from_slab(lax.broadcasted_iota(jnp.int32, (EXP * ROWS, ALL), 1))
        == lax.broadcasted_iota(jnp.int32, (EXP * ROWS, ALL), 0), 1.0, 0.0,
    ).astype(BF)
    back = jnp.where(
        from_slab(lax.broadcasted_iota(jnp.int32, (ALL, EXP * ROWS), 0))
        == lax.broadcasted_iota(jnp.int32, (ALL, EXP * ROWS), 1), 1.0, 0.0,
    ).astype(BF)

    net = Net(send, recv)
    pl.semaphore_wait(barrier, 8)
    go = net.go

    class Exchange:
        def __init__(self, rows, send_ref, arr_ref, via_ref, keep=None):
            for r in range(PLANES):
                part = rows[r * SLAB : (r + 1) * SLAB].astype(BF)
                if r == 0 and keep is None:
                    arr_ref[0] = part
                else:
                    send_ref[r] = part
            self.send, self.arr, self.via, self.keep = send_ref, arr_ref, via_ref, keep

        def start(self):
            lo, hi = pl.ds(0, HALF), pl.ds(HALF, HALF)
            self.first = go(self.send.at[2, :, hi], self.via, zs[3])
            self.copies = [go(self.send.at[2, :, lo], self.arr.at[2, :, lo], zs[2])]
            self.copies += [go(self.send.at[r], self.arr.at[PLANES - r], zs[r]) for r in (3, 1)]
            if self.keep is not None:
                self.own = pltpu.make_async_copy(self.send.at[0], self.arr.at[0], self.keep)
                self.own.start()

        def forward(self):
            got(self.first)
            self.copies.append(go(self.via, self.arr.at[2, :, pl.ds(HALF, HALF)], zs[3]))

        def finish(self):
            got(*self.copies)

    ex = Exchange(dot(picks[0] + picks[1], tok[...]), send_x, arr_x, via.at[0])
    ex.start()

    def weight(k, lo):
        return wgu.at[:, :, pl.ds(lo + k * FP, FP)]

    def down(k):
        return wdn.at[:, pl.ds(k * FP, FP), :]

    cross = [go(wg, weight(1, 0), xc), go(wu, weight(1, HID), xc), go(wd, down(1), xc)]
    side = [go(wg, weight(2, 0), cp), go(wu, weight(2, HID), cp), go(wd, down(2), cp)]

    cotf = cot[...].astype(F32)
    rows_d = [(jnp.sum(jnp.where(row_t == col_t, gw[k : k + 1, :], 0.0), axis=1, keepdims=True) * cotf).astype(BF) for k in range(2)]
    ed = Exchange(dot(picks[0], rows_d[0]) + dot(picks[1], rows_d[1]), send_d, arr_d, via.at[1])
    ex.forward()

    def chunk_in(arr_ref, g):
        rows = dot(into, arr_ref[...].reshape(ALL, D)).astype(BF)
        g[0, 0] = rows[:ROWS]
        g[1, 0] = rows[ROWS:]

    gx, gd = Gather(net, xg, xp, yu, yd), Gather(net, dg, xp, yu, yd)
    ex.finish()
    chunk_in(arr_x, xg)
    gx.start()
    ed.start()
    gx.step2()
    ed.forward()
    ed.finish()
    chunk_in(arr_d, dg)
    gd.start()
    got(cross[0])
    side.append(go(weight(1, 0), weight(3, 0), cp))
    gx.step3()
    got(cross[1])
    side.append(go(weight(1, HID), weight(3, HID), cp))
    for copy in own:
        copy.wait()
    got(*side)

    def forward(e):
        def tile(n, _):
            cols = pl.ds(pl.multiple_of(n * 256, 256), 256)
            rows = xg[e].reshape(MINE, D)
            gate = dot(rows, wgu[e, :, cols])
            up = dot(rows, wgu[e, :, pl.ds(pl.multiple_of(n * 256 + HID, 256), 256)])
            sig = 1.0 / (1.0 + jnp.exp(-gate))
            act = gate * sig
            hid[e, :, cols] = (act * up).astype(BF)
            fac_b[e, :, cols] = act
            fac_a[e, :, cols] = up * sig * (1.0 + gate * (1.0 - sig))
            return 0

        lax.fori_loop(0, HID // 256, tile, 0)

    def project(e):
        def tile(n, _):
            cols = pl.ds(pl.multiple_of(n * 256, 256), 256)
            po[e, :, :, cols] = dot(hid[e], wdn[e, :, cols]).astype(BF).reshape(SLOTS, ROWS, 256)
            return 0

        lax.fori_loop(0, D // 256, tile, 0)

    gx.finish(0)
    forward(0)
    gd.step2()
    gx.finish(1)
    forward(1)
    gd.step3()
    got(cross[2])
    late = go(down(1), down(3), cp)
    got(late)
    ro = Reduce(net, po, near_o, far_o, across_o, xp, yu, yd)
    rv = Reduce(net, pv, near_v, far_v, across_v, xp, yu, yd)
    project(0)
    ro.start0()
    project(1)
    ro.start1()

    def backward(e):
        def tile(n, _):
            cols = pl.ds(pl.multiple_of(n * 256, 256), 256)
            dact = dot(dg[e].reshape(MINE, D), wdn[e, cols, :], (1, 1))
            dgu[e, :, cols] = (dact * fac_a[e, :, cols]).astype(BF)
            dgu[e, :, pl.ds(pl.multiple_of(n * 256 + HID, 256), 256)] = (dact * fac_b[e, :, cols]).astype(BF)
            return 0

        lax.fori_loop(0, HID // 256, tile, 0)

    def propagate(e):
        def tile(n, _):
            cols = pl.ds(pl.multiple_of(n * 256, 256), 256)
            part = dot(dgu[e], wgu[e, cols, :], (1, 1))
            pv[e, :, :, cols] = part.astype(BF).reshape(SLOTS, ROWS, 256)
            return 0

        lax.fori_loop(0, D // 256, tile, 0)

    def down_grad(e):
        def tile(n, _):
            cols = pl.ds(pl.multiple_of(n * 256, 256), 256)
            pd[e, cols, :] = dot(hid[e, :, cols], dg[e].reshape(MINE, D), (0, 0)).astype(BF)
            return 0

        lax.fori_loop(0, HID // 256, tile, 0)

    def up_grad(e):
        def tile(n, _):
            cols = pl.ds(pl.multiple_of(n * 256, 256), 256)
            pgu[e, cols, :] = dot(xg[e, :, :, cols].reshape(MINE, 256), dgu[e], (0, 0)).astype(BF)
            return 0

        lax.fori_loop(0, D // 256, tile, 0)

    pair = 2 * FP
    share, kept = {}, []

    def keep(src, dst):
        copy = pltpu.make_async_copy(src, dst, local.at[3 + len(kept)])
        copy.start()
        kept.append(copy)

    def share_down(e):
        share["d", e] = go(pd.at[e, pl.ds(pair, pair), :], rd.at[e], cp)

    def share_up(e):
        for i in range(2):
            share[i, e] = go(pgu.at[e, :, pl.ds(i * HID + pair, pair)], rgu.at[i, e], cp)

    far = []

    def send_down(e):
        got(share["d", e])
        pd[e, pl.ds(0, pair), :] = (pd[e, pl.ds(0, pair), :].astype(F32) + rd[e].astype(F32)).astype(BF)
        far.append(go(pd.at[e, pl.ds(FP, FP), :], far_d.at[e], xc))
        keep(pd.at[e, pl.ds(0, FP), :], sum_d.at[e])

    def send_up(e):
        for i in range(2):
            got(share[i, e])
            cols = pl.ds(i * HID, pair)
            pgu[e, :, cols] = (pgu[e, :, cols].astype(F32) + rgu[i, e].astype(F32)).astype(BF)
            far.append(go(pgu.at[e, :, pl.ds(i * HID + FP, FP)], far_gu.at[i, e], xc))
            keep(pgu.at[e, :, pl.ds(i * HID, FP)], sum_gu.at[i, e])

    gd.finish(0)
    backward(0)
    down_grad(0)
    share_down(0)
    gd.finish(1)
    backward(1)
    ro.step2()
    down_grad(1)
    share_down(1)
    send_down(0)
    up_grad(0)
    share_up(0)
    send_down(1)
    ro.step3()
    up_grad(1)
    share_up(1)
    send_up(0)
    propagate(0)
    rv.start0()
    send_up(1)
    propagate(1)
    rv.start1()
    eo = Exchange(dot(back, ro.step4()), send_o, arr_o, via.at[2], local.at[9])
    eo.start()
    rv.step2()
    eo.forward()
    rv.step3()
    ev = Exchange(dot(back, rv.step4()), send_v, arr_v, via.at[3], local.at[10])
    ev.start()
    eo.finish()
    ev.forward()
    ev.finish()
    got(*far)
    for copy in kept + [eo.own, ev.own]:
        copy.wait()
    for copy in net.all:
        copy.wait_send()


def finish(gw, pick, arr_o, arr_v, sum_d, sum_gu, far_d, far_gu, mixed, gtok, ggate, gup, gdown):
    eye = lax.broadcasted_iota(jnp.int32, (TOK, TOK), 0) == lax.broadcasted_iota(jnp.int32, (TOK, TOK), 1)
    rows = arr_o[...].reshape(ALL, D)
    total = jnp.zeros((TOK, D), F32)
    for k in range(2):
        weight = jnp.sum(jnp.where(eye, gw[k : k + 1, :], 0.0), axis=1, keepdims=True)
        total = total + weight * dot(pick[k], rows, (0, 0))
    mixed[...] = total.astype(BF)
    gtok[...] = dot(pick[0] + pick[1], arr_v[...].reshape(ALL, D), (0, 0)).astype(BF)
    gdown[...] = (sum_d[...].astype(F32) + far_d[...].astype(F32)).astype(BF)
    ggate[...] = (sum_gu[0].astype(F32) + far_gu[0].astype(F32)).astype(BF)
    gup[...] = (sum_gu[1].astype(F32) + far_gu[1].astype(F32)).astype(BF)


def body(tokens, expert_ids, gate_weights, w_gate, w_up, w_down, cotangent):
    vmem, hbm = pl.BlockSpec(memory_space=pltpu.VMEM), pl.BlockSpec(memory_space=pl.ANY)

    def buf(*shape, dtype=BF):
        return pltpu.VMEM(shape, dtype)

    slab = [buf(PLANES, SLAB, D) for _ in range(6)]
    big = [buf(EXP, SLOTS, ROWS, D) for _ in range(4)]
    rings = [buf(3, 2, ROWS, HALF), buf(3, 2, ROWS, D), buf(5, ROWS, D)] * 2
    scratch = slab + [buf(4, SLAB, HALF)] + big + rings + [
        buf(EXP, D, 2 * HID), buf(EXP, HID, D),
        buf(EXP, MINE, HID, dtype=F32), buf(EXP, MINE, HID, dtype=F32),
        buf(EXP, MINE, HID), buf(EXP, MINE, 2 * HID),
        buf(EXP, HID, D), buf(EXP, D, 2 * HID),
        buf(EXP, 2 * FP, D), buf(2, EXP, D, 2 * FP),
        pltpu.SemaphoreType.DMA((COPIES,)), pltpu.SemaphoreType.DMA((COPIES,)), pltpu.SemaphoreType.DMA((11,)),
    ]

    def out(*shape):
        return jax.ShapeDtypeStruct(shape, BF)

    weights = gate_weights.T
    parts = pl.pallas_call(
        kernel,
        out_shape=(
            out(2, ALL, TOK), out(PLANES, SLAB, D), out(PLANES, SLAB, D),
            out(EXP, FP, D), out(2, EXP, D, FP), out(EXP, FP, D), out(2, EXP, D, FP),
        ),
        in_specs=[vmem] * 4 + [hbm] * 3,
        out_specs=(vmem,) + (hbm,) * 6,
        scratch_shapes=scratch,
        compiler_params=pltpu.CompilerParams(
            collective_id=0, has_side_effects=True, vmem_limit_bytes=67043328
        ),
    )(tokens, expert_ids.T, weights, cotangent, w_gate, w_up, w_down)
    return pl.pallas_call(
        finish,
        out_shape=tuple(
            jax.ShapeDtypeStruct(a.shape, BF) for a in (tokens, tokens, w_gate, w_up, w_down)
        ),
        in_specs=[vmem] * 8,
        out_specs=(vmem,) * 5,
    )(weights, *parts)


def solution(mesh):
    rows = P(("dp", "expert"), None)
    cols = P("expert", None, "dp")
    down = P("expert", "dp", None)
    return jax.shard_map(
        body,
        mesh=mesh,
        in_specs=(rows, rows, rows, cols, cols, down, rows),
        out_specs=(rows, rows, cols, cols, down),
        check_vma=False,
    )
```

```python
import jax
import jax.numpy as jnp
from jax import lax
from jax.experimental import pallas as pl
from jax.experimental.pallas import tpu as pltpu
from jax.sharding import PartitionSpec as P

MESH = pl.DeviceIdType.MESH
BF, F32 = jnp.bfloat16, jnp.float32
TOK, D, CAP = 64, 1024, 20
PLANES, EXP = 4, 2
SLAB = 48
ALL = PLANES * SLAB
ROWS = PLANES * CAP
SLOTS = 8
MINE = SLOTS * ROWS
HALF = D // 2
FP = 128
HID = 4 * FP
COPIES = 144


def dot(a, b, contract=(1, 0)):
    return lax.dot_general(a, b, (((contract[0],), (contract[1],)), ((), ())), preferred_element_type=F32)


class Net:
    def __init__(self, send, recv):
        self.send, self.recv, self.all = send, recv, []

    def go(self, src, dst, device):
        k = len(self.all)
        copy = pltpu.make_async_remote_copy(
            src_ref=src, dst_ref=dst, send_sem=self.send.at[k], recv_sem=self.recv.at[k],
            device_id=device, device_id_type=MESH,
        )
        copy.start()
        self.all.append(copy)
        return copy


def got(*copies):
    for copy in copies:
        copy.wait_recv()


def wide(u):
    return pl.ds(u * HALF, HALF)


def full(ref, u, s):
    return ref.at[:, s, :, wide(u)]


def half(ref, u, s, e):
    return ref.at[e, s, :, wide(u)]


class Gather:
    def __init__(self, net, ref, xp, yu, yd):
        self.net, self.ref, self.xp, self.yu, self.yd = net, ref, xp, yu, yd

    def move(self, u, src, dst, to):
        return self.net.go(full(self.ref, u, src), full(self.ref, u, dst), to)

    def pass_on(self, u, src, dst, e, to):
        return self.net.go(half(self.ref, u, src, e), half(self.ref, u, dst, e), to)

    def start0(self):
        self.x0 = self.move(0, 0, 4, self.xp)
        self.u00 = self.move(0, 0, 3, self.yu)
        self.d00 = self.move(0, 0, 1, self.yd)

    def start1(self):
        self.u1 = self.move(1, 0, 3, self.yu)
        self.d1 = self.move(1, 0, 1, self.yd)
        self.x1 = [self.move(1, 0, 4, self.xp)]

    def step2a(self):
        got(self.x0)
        self.u01 = self.move(0, 4, 7, self.yu)
        self.d01 = self.move(0, 4, 5, self.yd)

    def step2b(self):
        got(self.u1)
        self.fu1 = self.pass_on(1, 3, 2, 0, self.yu)
        self.x1.append(self.move(1, 3, 7, self.xp))
        got(self.d1)
        self.fd1 = self.pass_on(1, 1, 2, 1, self.yd)
        self.x1.append(self.move(1, 1, 5, self.xp))
        got(self.u00)
        self.fu00 = self.pass_on(0, 3, 2, 0, self.yu)
        got(self.d00)
        self.fd00 = self.pass_on(0, 1, 2, 1, self.yd)

    def step3(self):
        got(self.fu1, self.fd1)
        self.x1.append(self.move(1, 2, 6, self.xp))
        got(self.u01)
        self.fu01 = self.pass_on(0, 7, 6, 0, self.yu)
        got(self.d01)
        self.fd01 = self.pass_on(0, 5, 6, 1, self.yd)

    def finish(self):
        got(self.fu00, self.fd00, self.fu01, self.fd01)
        got(*self.x1)


class Reduce:
    def __init__(self, net, part, near, far, across, xp, yu, yd):
        self.net, self.p, self.near, self.far, self.across = net, part, near, far, across
        self.xp, self.yu, self.yd = xp, yu, yd
        self.ring = {}

    def outer(self, key, u, b):
        self.ring[key] = [
            self.net.go(half(self.p, u, b + 2, 0), self.near.at[key, 0], self.yu),
            self.net.go(half(self.p, u, b + 2, 1), self.near.at[key, 1], self.yd),
        ]

    def free_up(self, key, u, b):
        self.ring[key].append(self.net.go(half(self.p, u, b + 1, 1), self.far.at[key, 0, 1], self.yu))

    def free_down(self, key, u, b):
        self.ring[key].append(self.net.go(half(self.p, u, b + 3, 0), self.far.at[key, 1, 0], self.yd))

    def add(self, e, s, u, arrived):
        cols = wide(u)
        self.p[e, s, :, cols] = (self.p[e, s, :, cols].astype(F32) + arrived.astype(F32)).astype(BF)

    def inner(self, key, u, b):
        got(self.ring[key][0])
        self.add(0, b + 1, u, self.near[key, 0])
        up = self.net.go(half(self.p, u, b + 1, 0), self.far.at[key, 0, 0], self.yu)
        got(self.ring[key][1])
        self.add(1, b + 3, u, self.near[key, 1])
        down = self.net.go(half(self.p, u, b + 3, 1), self.far.at[key, 1, 1], self.yd)
        self.ring[key] += [up, down]

    def total(self, key, u, b):
        got(*self.ring[key][2:])
        return self.p[:, b, :, wide(u)].astype(F32) + self.far[key, 0].astype(F32) + self.far[key, 1].astype(F32)

    def start0(self):
        for dx in (1, 0):
            self.outer(dx, 0, 4 * dx)
        for dx in (1, 0):
            self.free_up(dx, 0, 4 * dx)
            self.free_down(dx, 0, 4 * dx)

    def start1(self):
        self.x1 = {dy: self.net.go(full(self.p, 1, 4 + dy), self.across.at[dy], self.xp) for dy in (2, 1, 3, 0)}

    def joined(self, dy):
        got(self.x1[dy])
        for e in range(EXP):
            self.add(e, dy, 1, self.across[dy, e])

    def step_a(self):
        self.joined(2)
        self.outer(2, 1, 0)
        self.inner(1, 0, 4)

    def step_b(self):
        self.inner(0, 0, 0)
        self.joined(1)
        self.free_up(2, 1, 0)

    def step_c(self):
        self.p[:, 4, :, wide(0)] = self.total(1, 0, 4).astype(BF)
        self.x0 = self.net.go(full(self.p, 0, 4), self.across.at[4], self.xp)
        self.joined(3)
        self.free_down(2, 1, 0)
        self.inner(2, 1, 0)

    def final0(self):
        rows = self.total(0, 0, 0)
        got(self.x0)
        return (rows + self.across[4].astype(F32)).astype(BF).reshape(EXP * ROWS, HALF)

    def final1(self):
        self.joined(0)
        return self.total(2, 1, 0).astype(BF).reshape(EXP * ROWS, HALF)


def kernel(
    tok, ids, gw, cot, wg, wu, wd,
    pick, arr_o, arr_v, sum_d, sum_gu, far_d, far_gu,
    send_x, send_d, send_o, send_v, arr_x, arr_d, via,
    xg, dg, po, pv, near_o, far_o, across_o, near_v, far_v, across_v,
    wgu, wdn, fac_a, fac_b, hid, dgu, pd, pgu, rd, rgu,
    send, recv, local,
):
    dp, z = lax.axis_index("dp"), lax.axis_index("expert")
    core, x, y = dp % 2, (dp // 2) % 4, dp // 8

    def at(yy, xx, cc):
        return ((yy * 4 + xx) * 2 + cc, z)

    xp = at(y, x + 1 - 2 * (x % 2), core)
    xc = at(y, 3 - x, core)
    yu, yd = at((y + 1) % 4, x, core), at((y + 3) % 4, x, core)
    cp = at(y, x, 1 - core)
    zs = {r: (dp, (z + r) % 4) for r in (1, 2, 3)}

    barrier = pltpu.get_barrier_semaphore()
    for device in (xp, xc, yu, yd, cp, zs[1], zs[2], zs[3]):
        pl.semaphore_signal(barrier, inc=1, device_id=device, device_id_type=MESH)

    own = [
        pltpu.make_async_copy(wg, wgu.at[:, :, pl.ds(0, FP)], local.at[0]),
        pltpu.make_async_copy(wu, wgu.at[:, :, pl.ds(HID, FP)], local.at[1]),
        pltpu.make_async_copy(wd, wdn.at[:, pl.ds(0, FP), :], local.at[2]),
    ]
    for copy in own:
        copy.start()

    expert = lax.broadcasted_iota(jnp.int32, (2 * PLANES, TOK), 0)
    hot = [jnp.where(expert == ids[k : k + 1, :], 1.0, 0.0) for k in range(2)]
    row_t = lax.broadcasted_iota(jnp.int32, (TOK, TOK), 0)
    col_t = lax.broadcasted_iota(jnp.int32, (TOK, TOK), 1)
    before = dot((hot[0] + hot[1]).astype(BF), jnp.where(row_t < col_t, 1.0, 0.0).astype(BF))
    slab_row = lax.broadcasted_iota(jnp.int32, (ALL, TOK), 0).astype(F32)
    picks = []
    for k in range(2):
        e = ids[k : k + 1, :]
        plane = lax.shift_right_logical(e, 1)
        rel = plane - z
        rel = jnp.where(rel < 0, rel + PLANES, rel)
        base = rel * SLAB + (e - 2 * plane) * CAP
        place = jnp.sum(hot[k] * before, axis=0, keepdims=True)
        picks.append(jnp.where(slab_row == base.astype(F32) + place, 1.0, 0.0).astype(BF))
        pick[k] = picks[k]

    def from_slab(c):
        s = (c >= SLAB).astype(jnp.int32) + (c >= 2 * SLAB).astype(jnp.int32) + (c >= 3 * SLAB).astype(jnp.int32)
        rest = c - SLAB * s
        j = (rest >= CAP).astype(jnp.int32)
        row = j * ROWS + s * CAP + rest - CAP * j
        return jnp.where(rest < EXP * CAP, row, -1)

    into = jnp.where(
        from_slab(lax.broadcasted_iota(jnp.int32, (EXP * ROWS, ALL), 1))
        == lax.broadcasted_iota(jnp.int32, (EXP * ROWS, ALL), 0), 1.0, 0.0,
    ).astype(BF)
    back = jnp.where(
        from_slab(lax.broadcasted_iota(jnp.int32, (ALL, EXP * ROWS), 0))
        == lax.broadcasted_iota(jnp.int32, (ALL, EXP * ROWS), 1), 1.0, 0.0,
    ).astype(BF)

    net = Net(send, recv)
    pl.semaphore_wait(barrier, 8)
    go = net.go

    class Exchange:
        def __init__(self, send_ref, arr_ref, via_ref, keep=None):
            self.send, self.arr, self.via, self.keep = send_ref, arr_ref, via_ref, keep
            self.first, self.copies, self.own = {}, {}, []

        def fill(self, rows, *units):
            for r in range(PLANES):
                part = rows[r * SLAB : (r + 1) * SLAB].astype(BF)
                ref = self.arr if r == 0 and self.keep is None else self.send
                if len(units) == 2:
                    ref[r] = part
                else:
                    ref[r, :, wide(units[0])] = part

        def start(self, u):
            lo, hi = pl.ds(u * HALF, HALF // 2), pl.ds(u * HALF + HALF // 2, HALF // 2)
            self.first[u] = go(self.send.at[2, :, hi], self.via.at[u], zs[3])
            self.copies[u] = [go(self.send.at[2, :, lo], self.arr.at[2, :, lo], zs[2])]
            self.copies[u] += [go(self.send.at[r, :, wide(u)], self.arr.at[PLANES - r, :, wide(u)], zs[r]) for r in (3, 1)]
            if self.keep is not None:
                own = pltpu.make_async_copy(self.send.at[0, :, wide(u)], self.arr.at[0, :, wide(u)], self.keep.at[u])
                own.start()
                self.own.append(own)

        def forward(self, u):
            got(self.first[u])
            hi = pl.ds(u * HALF + HALF // 2, HALF // 2)
            self.copies[u].append(go(self.via.at[u], self.arr.at[2, :, hi], zs[3]))

        def finish(self, u):
            got(*self.copies[u])

    ex = Exchange(send_x, arr_x, via.at[0])
    ex.fill(dot(picks[0] + picks[1], tok[...]), 0, 1)
    ex.start(0)
    ex.start(1)

    def weight(k, lo):
        return wgu.at[:, :, pl.ds(lo + k * FP, FP)]

    def down(k):
        return wdn.at[:, pl.ds(k * FP, FP), :]

    cross = [go(wg, weight(1, 0), xc), go(wu, weight(1, HID), xc), go(wd, down(1), xc)]
    side = [go(wg, weight(2, 0), cp), go(wu, weight(2, HID), cp), go(wd, down(2), cp)]

    cotf = cot[...].astype(F32)
    rows_d = [(jnp.sum(jnp.where(row_t == col_t, gw[k : k + 1, :], 0.0), axis=1, keepdims=True) * cotf).astype(BF) for k in range(2)]
    ed = Exchange(send_d, arr_d, via.at[1])
    ed.fill(dot(picks[0], rows_d[0]) + dot(picks[1], rows_d[1]), 0, 1)

    def chunk_in(arr_ref, g, u):
        rows = dot(into, arr_ref[:, :, wide(u)].reshape(ALL, HALF)).astype(BF)
        g[0, 0, :, wide(u)] = rows[:ROWS]
        g[1, 0, :, wide(u)] = rows[ROWS:]

    gx, gd = Gather(net, xg, xp, yu, yd), Gather(net, dg, xp, yu, yd)
    ex.forward(0)
    ex.finish(0)
    chunk_in(arr_x, xg, 0)
    gx.start0()
    ex.forward(1)
    ex.finish(1)
    chunk_in(arr_x, xg, 1)
    gx.start1()
    ed.start(0)
    ed.start(1)
    gx.step2a()
    ed.forward(0)
    ed.forward(1)
    gx.step2b()
    ed.finish(0)
    ed.finish(1)
    chunk_in(arr_d, dg, 0)
    chunk_in(arr_d, dg, 1)
    gd.start0()
    gd.start1()
    got(cross[0])
    side.append(go(weight(1, 0), weight(3, 0), cp))
    gx.step3()
    got(cross[1])
    side.append(go(weight(1, HID), weight(3, HID), cp))
    for copy in own:
        copy.wait()
    got(*side)

    def forward(e):
        def tile(n, _):
            cols = pl.ds(pl.multiple_of(n * 256, 256), 256)
            rows = xg[e].reshape(MINE, D)
            gate = dot(rows, wgu[e, :, cols])
            up = dot(rows, wgu[e, :, pl.ds(pl.multiple_of(n * 256 + HID, 256), 256)])
            sig = 1.0 / (1.0 + jnp.exp(-gate))
            act = gate * sig
            hid[e, :, cols] = (act * up).astype(BF)
            fac_b[e, :, cols] = act
            fac_a[e, :, cols] = up * sig * (1.0 + gate * (1.0 - sig))
            return 0

        lax.fori_loop(0, HID // 256, tile, 0)

    def project(u):
        def tile(i, _):
            e, cols = i // 2, pl.ds(pl.multiple_of(u * HALF + (i % 2) * 256, 256), 256)
            po[e, :, :, cols] = dot(hid[e], wdn[e, :, cols]).astype(BF).reshape(SLOTS, ROWS, 256)
            return 0

        lax.fori_loop(0, 2 * EXP, tile, 0)

    gx.finish()
    forward(0)
    gd.step2a()
    gd.step2b()
    forward(1)
    gd.step3()
    got(cross[2])
    late = go(down(1), down(3), cp)
    got(late)
    ro = Reduce(net, po, near_o, far_o, across_o, xp, yu, yd)
    rv = Reduce(net, pv, near_v, far_v, across_v, xp, yu, yd)
    project(1)
    ro.start1()
    project(0)
    ro.start0()

    def backward(e):
        def tile(n, _):
            cols = pl.ds(pl.multiple_of(n * 256, 256), 256)
            dact = dot(dg[e].reshape(MINE, D), wdn[e, cols, :], (1, 1))
            dgu[e, :, cols] = (dact * fac_a[e, :, cols]).astype(BF)
            dgu[e, :, pl.ds(pl.multiple_of(n * 256 + HID, 256), 256)] = (dact * fac_b[e, :, cols]).astype(BF)
            return 0

        lax.fori_loop(0, HID // 256, tile, 0)

    def propagate(u):
        def tile(i, _):
            e, cols = i // 2, pl.ds(pl.multiple_of(u * HALF + (i % 2) * 256, 256), 256)
            part = dot(dgu[e], wgu[e, cols, :], (1, 1))
            pv[e, :, :, cols] = part.astype(BF).reshape(SLOTS, ROWS, 256)
            return 0

        lax.fori_loop(0, 2 * EXP, tile, 0)

    def down_grad(e):
        def tile(n, _):
            cols = pl.ds(pl.multiple_of(n * 256, 256), 256)
            pd[e, cols, :] = dot(hid[e, :, cols], dg[e].reshape(MINE, D), (0, 0)).astype(BF)
            return 0

        lax.fori_loop(0, HID // 256, tile, 0)

    def up_grad(e):
        def tile(n, _):
            cols = pl.ds(pl.multiple_of(n * 256, 256), 256)
            pgu[e, cols, :] = dot(xg[e, :, :, cols].reshape(MINE, 256), dgu[e], (0, 0)).astype(BF)
            return 0

        lax.fori_loop(0, D // 256, tile, 0)

    pair = 2 * FP
    share, kept = {}, []

    def keep(src, dst):
        copy = pltpu.make_async_copy(src, dst, local.at[3 + len(kept)])
        copy.start()
        kept.append(copy)

    def share_down(e):
        share["d", e] = go(pd.at[e, pl.ds(pair, pair), :], rd.at[e], cp)

    def share_up(e):
        for i in range(2):
            share[i, e] = go(pgu.at[e, :, pl.ds(i * HID + pair, pair)], rgu.at[i, e], cp)

    far = []

    def send_down(e):
        got(share["d", e])
        pd[e, pl.ds(0, pair), :] = (pd[e, pl.ds(0, pair), :].astype(F32) + rd[e].astype(F32)).astype(BF)
        far.append(go(pd.at[e, pl.ds(FP, FP), :], far_d.at[e], xc))
        keep(pd.at[e, pl.ds(0, FP), :], sum_d.at[e])

    def send_up(e):
        for i in range(2):
            got(share[i, e])
            cols = pl.ds(i * HID, pair)
            pgu[e, :, cols] = (pgu[e, :, cols].astype(F32) + rgu[i, e].astype(F32)).astype(BF)
            far.append(go(pgu.at[e, :, pl.ds(i * HID + FP, FP)], far_gu.at[i, e], xc))
            keep(pgu.at[e, :, pl.ds(i * HID, FP)], sum_gu.at[i, e])

    gd.finish()
    down_grad(0)
    share_down(0)
    backward(0)
    ro.step_a()
    down_grad(1)
    share_down(1)
    send_down(0)
    backward(1)
    send_down(1)
    ro.step_b()
    up_grad(0)
    share_up(0)
    ro.step_c()
    propagate(1)
    rv.start1()
    send_up(0)
    propagate(0)
    rv.start0()
    eo = Exchange(send_o, arr_o, via.at[2], local.at[pl.ds(9, 2)])
    ev = Exchange(send_v, arr_v, via.at[3], local.at[pl.ds(11, 2)])
    up_grad(1)
    share_up(1)
    eo.fill(dot(back, ro.final1()), 1)
    eo.start(1)
    eo.fill(dot(back, ro.final0()), 0)
    eo.start(0)
    send_up(1)
    rv.step_a()
    eo.forward(1)
    eo.forward(0)
    rv.step_b()
    rv.step_c()
    ev.fill(dot(back, rv.final1()), 1)
    ev.start(1)
    ev.fill(dot(back, rv.final0()), 0)
    ev.start(0)
    ev.forward(1)
    ev.forward(0)
    for u in range(2):
        eo.finish(u)
        ev.finish(u)
    got(*far)
    for copy in kept + eo.own + ev.own:
        copy.wait()
    for copy in net.all:
        copy.wait_send()


def finish(gw, pick, arr_o, arr_v, sum_d, sum_gu, far_d, far_gu, mixed, gtok, ggate, gup, gdown):
    eye = lax.broadcasted_iota(jnp.int32, (TOK, TOK), 0) == lax.broadcasted_iota(jnp.int32, (TOK, TOK), 1)
    rows = arr_o[...].reshape(ALL, D)
    total = jnp.zeros((TOK, D), F32)
    for k in range(2):
        weight = jnp.sum(jnp.where(eye, gw[k : k + 1, :], 0.0), axis=1, keepdims=True)
        total = total + weight * dot(pick[k], rows, (0, 0))
    mixed[...] = total.astype(BF)
    gtok[...] = dot(pick[0] + pick[1], arr_v[...].reshape(ALL, D), (0, 0)).astype(BF)
    gdown[...] = (sum_d[...].astype(F32) + far_d[...].astype(F32)).astype(BF)
    ggate[...] = (sum_gu[0].astype(F32) + far_gu[0].astype(F32)).astype(BF)
    gup[...] = (sum_gu[1].astype(F32) + far_gu[1].astype(F32)).astype(BF)


def body(tokens, expert_ids, gate_weights, w_gate, w_up, w_down, cotangent):
    vmem, hbm = pl.BlockSpec(memory_space=pltpu.VMEM), pl.BlockSpec(memory_space=pl.ANY)

    def buf(*shape, dtype=BF):
        return pltpu.VMEM(shape, dtype)

    slab = [buf(PLANES, SLAB, D) for _ in range(6)]
    big = [buf(EXP, SLOTS, ROWS, D) for _ in range(4)]
    rings = [buf(3, 2, ROWS, HALF), buf(3, 2, EXP, ROWS, HALF), buf(5, EXP, ROWS, HALF)] * 2
    scratch = slab + [buf(4, 2, SLAB, HALF // 2)] + big + rings + [
        buf(EXP, D, 2 * HID), buf(EXP, HID, D),
        buf(EXP, MINE, HID, dtype=F32), buf(EXP, MINE, HID, dtype=F32),
        buf(EXP, MINE, HID), buf(EXP, MINE, 2 * HID),
        buf(EXP, HID, D), buf(EXP, D, 2 * HID),
        buf(EXP, 2 * FP, D), buf(2, EXP, D, 2 * FP),
        pltpu.SemaphoreType.DMA((COPIES,)), pltpu.SemaphoreType.DMA((COPIES,)), pltpu.SemaphoreType.DMA((13,)),
    ]

    def out(*shape):
        return jax.ShapeDtypeStruct(shape, BF)

    weights = gate_weights.T
    parts = pl.pallas_call(
        kernel,
        out_shape=(
            out(2, ALL, TOK), out(PLANES, SLAB, D), out(PLANES, SLAB, D),
            out(EXP, FP, D), out(2, EXP, D, FP), out(EXP, FP, D), out(2, EXP, D, FP),
        ),
        in_specs=[vmem] * 4 + [hbm] * 3,
        out_specs=(vmem,) + (hbm,) * 6,
        scratch_shapes=scratch,
        compiler_params=pltpu.CompilerParams(
            collective_id=0, has_side_effects=True, vmem_limit_bytes=67043328
        ),
    )(tokens, expert_ids.T, weights, cotangent, w_gate, w_up, w_down)
    return pl.pallas_call(
        finish,
        out_shape=tuple(
            jax.ShapeDtypeStruct(a.shape, BF) for a in (tokens, tokens, w_gate, w_up, w_down)
        ),
        in_specs=[vmem] * 8,
        out_specs=(vmem,) * 5,
    )(weights, *parts)


def solution(mesh):
    rows = P(("dp", "expert"), None)
    cols = P("expert", None, "dp")
    down = P("expert", "dp", None)
    return jax.shard_map(
        body,
        mesh=mesh,
        in_specs=(rows, rows, rows, cols, cols, down, rows),
        out_specs=(rows, rows, cols, cols, down),
        check_vma=False,
    )
```

```python
import jax
import jax.numpy as jnp
from jax import lax
from jax.experimental import pallas as pl
from jax.experimental.pallas import tpu as pltpu
from jax.sharding import PartitionSpec as P

MESH = pl.DeviceIdType.MESH
BF, F32 = jnp.bfloat16, jnp.float32
TOK, D, CAP = 64, 1024, 20
PLANES, EXP = 4, 2
SLAB = 48
ALL = PLANES * SLAB
ROWS = PLANES * CAP
SLOTS = 8
MINE = SLOTS * ROWS
HALF = D // 2
FP = 128
HID = 4 * FP
COPIES = 144


def dot(a, b, contract=(1, 0)):
    return lax.dot_general(a, b, (((contract[0],), (contract[1],)), ((), ())), preferred_element_type=F32)


class Net:
    def __init__(self, send, recv):
        self.send, self.recv, self.all = send, recv, []

    def go(self, src, dst, device):
        k = len(self.all)
        copy = pltpu.make_async_remote_copy(
            src_ref=src, dst_ref=dst, send_sem=self.send.at[k], recv_sem=self.recv.at[k],
            device_id=device, device_id_type=MESH,
        )
        copy.start()
        self.all.append(copy)
        return copy


def got(*copies):
    for copy in copies:
        copy.wait_recv()


def wide(u):
    return pl.ds(u * HALF, HALF)


def full(ref, u, s):
    return ref.at[:, s, :, wide(u)]


def half(ref, u, s, e):
    return ref.at[e, s, :, wide(u)]


class Gather:
    def __init__(self, net, ref, xp, yu, yd):
        self.net, self.ref, self.xp, self.yu, self.yd = net, ref, xp, yu, yd

    def move(self, u, src, dst, to):
        return self.net.go(full(self.ref, u, src), full(self.ref, u, dst), to)

    def pass_on(self, u, src, dst, e, to):
        return self.net.go(half(self.ref, u, src, e), half(self.ref, u, dst, e), to)

    def start0(self):
        self.x0 = self.move(0, 0, 4, self.xp)
        self.u00 = self.move(0, 0, 3, self.yu)
        self.d00 = self.move(0, 0, 1, self.yd)

    def start1(self):
        self.u1 = self.move(1, 0, 3, self.yu)
        self.d1 = self.move(1, 0, 1, self.yd)
        self.x1 = [self.move(1, 0, 4, self.xp)]

    def step2a(self):
        got(self.x0)
        self.u01 = self.move(0, 4, 7, self.yu)
        self.d01 = self.move(0, 4, 5, self.yd)

    def step2b(self):
        got(self.u1)
        self.fu1 = self.pass_on(1, 3, 2, 0, self.yu)
        self.x1.append(self.move(1, 3, 7, self.xp))
        got(self.d1)
        self.fd1 = self.pass_on(1, 1, 2, 1, self.yd)
        self.x1.append(self.move(1, 1, 5, self.xp))
        got(self.u00)
        self.fu00 = self.pass_on(0, 3, 2, 0, self.yu)
        got(self.d00)
        self.fd00 = self.pass_on(0, 1, 2, 1, self.yd)

    def step3(self):
        got(self.fu1, self.fd1)
        self.x1.append(self.move(1, 2, 6, self.xp))
        got(self.u01)
        self.fu01 = self.pass_on(0, 7, 6, 0, self.yu)
        got(self.d01)
        self.fd01 = self.pass_on(0, 5, 6, 1, self.yd)

    def finish(self):
        got(self.fu00, self.fd00, self.fu01, self.fd01)
        got(*self.x1)


class Reduce:
    def __init__(self, net, part, near, far, across, xp, yu, yd):
        self.net, self.p, self.near, self.far, self.across = net, part, near, far, across
        self.xp, self.yu, self.yd = xp, yu, yd
        self.ring = {}

    def outer(self, key, u, b):
        self.ring[key] = [
            self.net.go(half(self.p, u, b + 2, 0), self.near.at[key, 0], self.yu),
            self.net.go(half(self.p, u, b + 2, 1), self.near.at[key, 1], self.yd),
        ]

    def free_up(self, key, u, b):
        self.ring[key].append(self.net.go(half(self.p, u, b + 1, 1), self.far.at[key, 0, 1], self.yu))

    def free_down(self, key, u, b):
        self.ring[key].append(self.net.go(half(self.p, u, b + 3, 0), self.far.at[key, 1, 0], self.yd))

    def add(self, e, s, u, arrived):
        cols = wide(u)
        self.p[e, s, :, cols] = (self.p[e, s, :, cols].astype(F32) + arrived.astype(F32)).astype(BF)

    def inner(self, key, u, b):
        got(self.ring[key][0])
        self.add(0, b + 1, u, self.near[key, 0])
        up = self.net.go(half(self.p, u, b + 1, 0), self.far.at[key, 0, 0], self.yu)
        got(self.ring[key][1])
        self.add(1, b + 3, u, self.near[key, 1])
        down = self.net.go(half(self.p, u, b + 3, 1), self.far.at[key, 1, 1], self.yd)
        self.ring[key] += [up, down]

    def total(self, key, u, b):
        got(*self.ring[key][2:])
        return self.p[:, b, :, wide(u)].astype(F32) + self.far[key, 0].astype(F32) + self.far[key, 1].astype(F32)

    def start0(self):
        for dx in (1, 0):
            self.outer(dx, 0, 4 * dx)
        for dx in (1, 0):
            self.free_up(dx, 0, 4 * dx)
            self.free_down(dx, 0, 4 * dx)

    def start1(self):
        self.x1 = {dy: self.net.go(full(self.p, 1, 4 + dy), self.across.at[dy], self.xp) for dy in (2, 1, 3, 0)}

    def joined(self, dy):
        got(self.x1[dy])
        for e in range(EXP):
            self.add(e, dy, 1, self.across[dy, e])

    def step_a(self):
        self.joined(2)
        self.outer(2, 1, 0)
        self.inner(1, 0, 4)

    def step_b(self):
        self.inner(0, 0, 0)
        self.joined(1)
        self.free_up(2, 1, 0)

    def step_c(self):
        self.p[:, 4, :, wide(0)] = self.total(1, 0, 4).astype(BF)
        self.x0 = self.net.go(full(self.p, 0, 4), self.across.at[4], self.xp)
        self.joined(3)
        self.free_down(2, 1, 0)
        self.inner(2, 1, 0)

    def final0(self):
        rows = self.total(0, 0, 0)
        got(self.x0)
        return (rows + self.across[4].astype(F32)).astype(BF).reshape(EXP * ROWS, HALF)

    def final1(self):
        self.joined(0)
        return self.total(2, 1, 0).astype(BF).reshape(EXP * ROWS, HALF)


def kernel(
    ids, gw, tok_in, cot_in, wg, wu, wd,
    pick_out, arr_o, arr_v, sum_d, sum_gu, far_d, far_gu,
    send_x, send_d, send_o, send_v, arr_x, arr_d, via,
    xg, dg, po, pv, near_o, far_o, across_o, near_v, far_v, across_v,
    tok, cot, pick, wgu, wdn, fac_a, fac_b, hid, dgu, pd, pgu, rd, rgu,
    send, recv, local,
):
    dp, z = lax.axis_index("dp"), lax.axis_index("expert")
    core, x, y = dp % 2, (dp // 2) % 4, dp // 8

    def at(yy, xx, cc):
        return ((yy * 4 + xx) * 2 + cc, z)

    xp = at(y, x + 1 - 2 * (x % 2), core)
    xc = at(y, 3 - x, core)
    yu, yd = at((y + 1) % 4, x, core), at((y + 3) % 4, x, core)
    cp = at(y, x, 1 - core)
    zs = {r: (dp, (z + r) % 4) for r in (1, 2, 3)}

    barrier = pltpu.get_barrier_semaphore()
    for device in (xp, xc, yu, yd, cp, zs[1], zs[2], zs[3]):
        pl.semaphore_signal(barrier, inc=1, device_id=device, device_id_type=MESH)

    tokens_in = [pltpu.make_async_copy(tok_in, tok, local.at[13]), pltpu.make_async_copy(cot_in, cot, local.at[14])]
    own = [
        pltpu.make_async_copy(wg, wgu.at[:, :, pl.ds(0, FP)], local.at[0]),
        pltpu.make_async_copy(wu, wgu.at[:, :, pl.ds(HID, FP)], local.at[1]),
        pltpu.make_async_copy(wd, wdn.at[:, pl.ds(0, FP), :], local.at[2]),
    ]
    for copy in tokens_in + own:
        copy.start()

    expert = lax.broadcasted_iota(jnp.int32, (2 * PLANES, TOK), 0)
    hot = [jnp.where(expert == ids[k : k + 1, :], 1.0, 0.0) for k in range(2)]
    row_t = lax.broadcasted_iota(jnp.int32, (TOK, TOK), 0)
    col_t = lax.broadcasted_iota(jnp.int32, (TOK, TOK), 1)
    before = dot((hot[0] + hot[1]).astype(BF), jnp.where(row_t < col_t, 1.0, 0.0).astype(BF))
    slab_row = lax.broadcasted_iota(jnp.int32, (ALL, TOK), 0).astype(F32)
    picks = []
    for k in range(2):
        e = ids[k : k + 1, :]
        plane = lax.shift_right_logical(e, 1)
        rel = plane - z
        rel = jnp.where(rel < 0, rel + PLANES, rel)
        base = rel * SLAB + (e - 2 * plane) * CAP
        place = jnp.sum(hot[k] * before, axis=0, keepdims=True)
        picks.append(jnp.where(slab_row == base.astype(F32) + place, 1.0, 0.0).astype(BF))
        pick[k] = picks[k]

    net = Net(send, recv)
    go = net.go

    class Exchange:
        def __init__(self, send_ref, arr_ref, via_ref, keep=None):
            self.send, self.arr, self.via, self.keep = send_ref, arr_ref, via_ref, keep
            self.first, self.copies, self.own = {}, {}, []

        def fill(self, rows, *units):
            for r in range(PLANES):
                part = rows[r * SLAB : (r + 1) * SLAB].astype(BF)
                ref = self.arr if r == 0 and self.keep is None else self.send
                if len(units) == 2:
                    ref[r] = part
                else:
                    ref[r, :, wide(units[0])] = part

        def start(self, u):
            lo, hi = pl.ds(u * HALF, HALF // 2), pl.ds(u * HALF + HALF // 2, HALF // 2)
            self.first[u] = go(self.send.at[2, :, hi], self.via.at[u], zs[3])
            self.copies[u] = [go(self.send.at[2, :, lo], self.arr.at[2, :, lo], zs[2])]
            self.copies[u] += [go(self.send.at[r, :, wide(u)], self.arr.at[PLANES - r, :, wide(u)], zs[r]) for r in (3, 1)]
            if self.keep is not None:
                own = pltpu.make_async_copy(self.send.at[0, :, wide(u)], self.arr.at[0, :, wide(u)], self.keep.at[u])
                own.start()
                self.own.append(own)

        def forward(self, u):
            got(self.first[u])
            hi = pl.ds(u * HALF + HALF // 2, HALF // 2)
            self.copies[u].append(go(self.via.at[u], self.arr.at[2, :, hi], zs[3]))

        def finish(self, u):
            got(*self.copies[u])

    ex = Exchange(send_x, arr_x, via.at[0])
    tokens_in[0].wait()
    ex.fill(dot(picks[0] + picks[1], tok[...]), 0, 1)
    pl.semaphore_wait(barrier, 8)
    ex.start(0)
    ex.start(1)

    def weight(k, lo):
        return wgu.at[:, :, pl.ds(lo + k * FP, FP)]

    def down(k):
        return wdn.at[:, pl.ds(k * FP, FP), :]

    cross = [go(wg, weight(1, 0), xc), go(wu, weight(1, HID), xc), go(wd, down(1), xc)]
    side = [go(wg, weight(2, 0), cp), go(wu, weight(2, HID), cp), go(wd, down(2), cp)]

    tokens_in[1].wait()
    cotf = cot[...].astype(F32)
    rows_d = [(jnp.sum(jnp.where(row_t == col_t, gw[k : k + 1, :], 0.0), axis=1, keepdims=True) * cotf).astype(BF) for k in range(2)]
    ed = Exchange(send_d, arr_d, via.at[1])
    ed.fill(dot(picks[0], rows_d[0]) + dot(picks[1], rows_d[1]), 0, 1)

    def from_slab(c):
        s = (c >= SLAB).astype(jnp.int32) + (c >= 2 * SLAB).astype(jnp.int32) + (c >= 3 * SLAB).astype(jnp.int32)
        rest = c - SLAB * s
        j = (rest >= CAP).astype(jnp.int32)
        row = j * ROWS + s * CAP + rest - CAP * j
        return jnp.where(rest < EXP * CAP, row, -1)

    into = jnp.where(
        from_slab(lax.broadcasted_iota(jnp.int32, (EXP * ROWS, ALL), 1))
        == lax.broadcasted_iota(jnp.int32, (EXP * ROWS, ALL), 0), 1.0, 0.0,
    ).astype(BF)
    back = jnp.where(
        from_slab(lax.broadcasted_iota(jnp.int32, (ALL, EXP * ROWS), 0))
        == lax.broadcasted_iota(jnp.int32, (ALL, EXP * ROWS), 1), 1.0, 0.0,
    ).astype(BF)

    def chunk_in(arr_ref, g, u):
        rows = dot(into, arr_ref[:, :, wide(u)].reshape(ALL, HALF)).astype(BF)
        g[0, 0, :, wide(u)] = rows[:ROWS]
        g[1, 0, :, wide(u)] = rows[ROWS:]

    gx, gd = Gather(net, xg, xp, yu, yd), Gather(net, dg, xp, yu, yd)
    ex.forward(0)
    ex.finish(0)
    chunk_in(arr_x, xg, 0)
    gx.start0()
    ex.forward(1)
    ex.finish(1)
    chunk_in(arr_x, xg, 1)
    gx.start1()
    ed.start(0)
    ed.start(1)
    gx.step2a()
    ed.forward(0)
    ed.forward(1)
    gx.step2b()
    ed.finish(0)
    ed.finish(1)
    chunk_in(arr_d, dg, 0)
    chunk_in(arr_d, dg, 1)
    gd.start0()
    gd.start1()
    got(cross[0])
    side.append(go(weight(1, 0), weight(3, 0), cp))
    gx.step3()
    got(cross[1])
    side.append(go(weight(1, HID), weight(3, HID), cp))
    for copy in own:
        copy.wait()
    got(*side)

    def forward(e):
        def tile(n, _):
            cols = pl.ds(pl.multiple_of(n * 256, 256), 256)
            rows = xg[e].reshape(MINE, D)
            gate = dot(rows, wgu[e, :, cols])
            up = dot(rows, wgu[e, :, pl.ds(pl.multiple_of(n * 256 + HID, 256), 256)])
            sig = 1.0 / (1.0 + jnp.exp(-gate))
            act = gate * sig
            hid[e, :, cols] = (act * up).astype(BF)
            fac_b[e, :, cols] = act
            fac_a[e, :, cols] = up * sig * (1.0 + gate * (1.0 - sig))
            return 0

        lax.fori_loop(0, HID // 256, tile, 0)

    def project(u):
        def tile(i, _):
            e, cols = i // 2, pl.ds(pl.multiple_of(u * HALF + (i % 2) * 256, 256), 256)
            po[e, :, :, cols] = dot(hid[e], wdn[e, :, cols]).astype(BF).reshape(SLOTS, ROWS, 256)
            return 0

        lax.fori_loop(0, 2 * EXP, tile, 0)

    gx.finish()
    forward(0)
    gd.step2a()
    gd.step2b()
    forward(1)
    gd.step3()
    got(cross[2])
    late = go(down(1), down(3), cp)
    got(late)
    ro = Reduce(net, po, near_o, far_o, across_o, xp, yu, yd)
    rv = Reduce(net, pv, near_v, far_v, across_v, xp, yu, yd)
    project(1)
    ro.start1()
    project(0)
    ro.start0()

    def backward(e):
        def tile(n, _):
            cols = pl.ds(pl.multiple_of(n * 256, 256), 256)
            dact = dot(dg[e].reshape(MINE, D), wdn[e, cols, :], (1, 1))
            dgu[e, :, cols] = (dact * fac_a[e, :, cols]).astype(BF)
            dgu[e, :, pl.ds(pl.multiple_of(n * 256 + HID, 256), 256)] = (dact * fac_b[e, :, cols]).astype(BF)
            return 0

        lax.fori_loop(0, HID // 256, tile, 0)

    def propagate(u):
        def tile(i, _):
            e, cols = i // 2, pl.ds(pl.multiple_of(u * HALF + (i % 2) * 256, 256), 256)
            part = dot(dgu[e], wgu[e, cols, :], (1, 1))
            pv[e, :, :, cols] = part.astype(BF).reshape(SLOTS, ROWS, 256)
            return 0

        lax.fori_loop(0, 2 * EXP, tile, 0)

    def down_grad(e):
        def tile(n, _):
            cols = pl.ds(pl.multiple_of(n * 256, 256), 256)
            pd[e, cols, :] = dot(hid[e, :, cols], dg[e].reshape(MINE, D), (0, 0)).astype(BF)
            return 0

        lax.fori_loop(0, HID // 256, tile, 0)

    def up_grad(e):
        def tile(n, _):
            cols = pl.ds(pl.multiple_of(n * 256, 256), 256)
            pgu[e, cols, :] = dot(xg[e, :, :, cols].reshape(MINE, 256), dgu[e], (0, 0)).astype(BF)
            return 0

        lax.fori_loop(0, D // 256, tile, 0)

    pair = 2 * FP
    share, kept = {}, []

    def keep(src, dst):
        copy = pltpu.make_async_copy(src, dst, local.at[3 + len(kept)])
        copy.start()
        kept.append(copy)

    def share_down(e):
        share["d", e] = go(pd.at[e, pl.ds(pair, pair), :], rd.at[e], cp)

    def share_up(e):
        for i in range(2):
            share[i, e] = go(pgu.at[e, :, pl.ds(i * HID + pair, pair)], rgu.at[i, e], cp)

    far = []

    def send_down(e):
        got(share["d", e])
        pd[e, pl.ds(0, pair), :] = (pd[e, pl.ds(0, pair), :].astype(F32) + rd[e].astype(F32)).astype(BF)
        far.append(go(pd.at[e, pl.ds(FP, FP), :], far_d.at[e], xc))
        keep(pd.at[e, pl.ds(0, FP), :], sum_d.at[e])

    def send_up(e):
        for i in range(2):
            got(share[i, e])
            cols = pl.ds(i * HID, pair)
            pgu[e, :, cols] = (pgu[e, :, cols].astype(F32) + rgu[i, e].astype(F32)).astype(BF)
            far.append(go(pgu.at[e, :, pl.ds(i * HID + FP, FP)], far_gu.at[i, e], xc))
            keep(pgu.at[e, :, pl.ds(i * HID, FP)], sum_gu.at[i, e])

    picks_out = pltpu.make_async_copy(pick, pick_out, local.at[15])
    picks_out.start()
    gd.finish()
    down_grad(0)
    share_down(0)
    backward(0)
    ro.step_a()
    down_grad(1)
    share_down(1)
    send_down(0)
    backward(1)
    send_down(1)
    ro.step_b()
    up_grad(0)
    share_up(0)
    ro.step_c()
    propagate(1)
    rv.start1()
    send_up(0)
    propagate(0)
    rv.start0()
    eo = Exchange(send_o, arr_o, via.at[2], local.at[pl.ds(9, 2)])
    ev = Exchange(send_v, arr_v, via.at[3], local.at[pl.ds(11, 2)])
    up_grad(1)
    share_up(1)
    eo.fill(dot(back, ro.final1()), 1)
    eo.start(1)
    eo.fill(dot(back, ro.final0()), 0)
    eo.start(0)
    send_up(1)
    rv.step_a()
    eo.forward(1)
    eo.forward(0)
    rv.step_b()
    rv.step_c()
    ev.fill(dot(back, rv.final1()), 1)
    ev.start(1)
    ev.fill(dot(back, rv.final0()), 0)
    ev.start(0)
    ev.forward(1)
    ev.forward(0)
    for u in range(2):
        eo.finish(u)
        ev.finish(u)
    got(*far)
    for copy in kept + eo.own + ev.own + [picks_out]:
        copy.wait()
    for copy in net.all:
        copy.wait_send()


def finish(gw, pick, arr_o, arr_v, sum_d, sum_gu, far_d, far_gu, mixed, gtok, ggate, gup, gdown):
    eye = lax.broadcasted_iota(jnp.int32, (TOK, TOK), 0) == lax.broadcasted_iota(jnp.int32, (TOK, TOK), 1)
    rows = arr_o[...].reshape(ALL, D)
    total = jnp.zeros((TOK, D), F32)
    for k in range(2):
        weight = jnp.sum(jnp.where(eye, gw[k : k + 1, :], 0.0), axis=1, keepdims=True)
        total = total + weight * dot(pick[k], rows, (0, 0))
    mixed[...] = total.astype(BF)
    gtok[...] = dot(pick[0] + pick[1], arr_v[...].reshape(ALL, D), (0, 0)).astype(BF)
    gdown[...] = (sum_d[...].astype(F32) + far_d[...].astype(F32)).astype(BF)
    ggate[...] = (sum_gu[0].astype(F32) + far_gu[0].astype(F32)).astype(BF)
    gup[...] = (sum_gu[1].astype(F32) + far_gu[1].astype(F32)).astype(BF)


def body(tokens, expert_ids, gate_weights, w_gate, w_up, w_down, cotangent):
    vmem, hbm = pl.BlockSpec(memory_space=pltpu.VMEM), pl.BlockSpec(memory_space=pl.ANY)

    def buf(*shape, dtype=BF):
        return pltpu.VMEM(shape, dtype)

    slab = [buf(PLANES, SLAB, D) for _ in range(6)]
    big = [buf(EXP, SLOTS, ROWS, D) for _ in range(4)]
    rings = [buf(3, 2, ROWS, HALF), buf(3, 2, EXP, ROWS, HALF), buf(5, EXP, ROWS, HALF)] * 2
    scratch = slab + [buf(4, 2, SLAB, HALF // 2)] + big + rings + [
        buf(TOK, D), buf(TOK, D), buf(2, ALL, TOK),
        buf(EXP, D, 2 * HID), buf(EXP, HID, D),
        buf(EXP, MINE, HID, dtype=F32), buf(EXP, MINE, HID, dtype=F32),
        buf(EXP, MINE, HID), buf(EXP, MINE, 2 * HID),
        buf(EXP, HID, D), buf(EXP, D, 2 * HID),
        buf(EXP, 2 * FP, D), buf(2, EXP, D, 2 * FP),
        pltpu.SemaphoreType.DMA((COPIES,)), pltpu.SemaphoreType.DMA((COPIES,)), pltpu.SemaphoreType.DMA((16,)),
    ]

    def out(*shape):
        return jax.ShapeDtypeStruct(shape, BF)

    weights = gate_weights.T
    parts = pl.pallas_call(
        kernel,
        out_shape=(
            out(2, ALL, TOK), out(PLANES, SLAB, D), out(PLANES, SLAB, D),
            out(EXP, FP, D), out(2, EXP, D, FP), out(EXP, FP, D), out(2, EXP, D, FP),
        ),
        in_specs=[vmem] * 2 + [hbm] * 5,
        out_specs=(hbm,) * 7,
        scratch_shapes=scratch,
        compiler_params=pltpu.CompilerParams(
            collective_id=0, has_side_effects=True, vmem_limit_bytes=67043328
        ),
    )(expert_ids.T, weights, tokens, cotangent, w_gate, w_up, w_down)
    return pl.pallas_call(
        finish,
        out_shape=tuple(
            jax.ShapeDtypeStruct(a.shape, BF) for a in (tokens, tokens, w_gate, w_up, w_down)
        ),
        in_specs=[vmem] * 8,
        out_specs=(vmem,) * 5,
    )(weights, *parts)


def solution(mesh):
    rows = P(("dp", "expert"), None)
    cols = P("expert", None, "dp")
    down = P("expert", "dp", None)
    return jax.shard_map(
        body,
        mesh=mesh,
        in_specs=(rows, rows, rows, cols, cols, down, rows),
        out_specs=(rows, rows, cols, cols, down),
        check_vma=False,
    )
```

```python
import jax
import jax.numpy as jnp
from jax import lax
from jax.experimental import pallas as pl
from jax.experimental.pallas import tpu as pltpu
from jax.sharding import PartitionSpec as P

MESH = pl.DeviceIdType.MESH
BF, F32 = jnp.bfloat16, jnp.float32
TOK, D, CAP = 64, 1024, 20
PLANES, EXP = 4, 2
SLAB = 48
ALL = PLANES * SLAB
ROWS = PLANES * CAP
SLOTS = 8
MINE = SLOTS * ROWS
HALF = D // 2
FP = 128
HID = 4 * FP
COPIES = 144


def dot(a, b, contract=(1, 0)):
    return lax.dot_general(a, b, (((contract[0],), (contract[1],)), ((), ())), preferred_element_type=F32)


class Net:
    def __init__(self, send, recv):
        self.send, self.recv, self.all = send, recv, []

    def go(self, src, dst, device):
        k = len(self.all)
        copy = pltpu.make_async_remote_copy(
            src_ref=src, dst_ref=dst, send_sem=self.send.at[k], recv_sem=self.recv.at[k],
            device_id=device, device_id_type=MESH,
        )
        copy.start()
        self.all.append(copy)
        return copy


def got(*copies):
    for copy in copies:
        copy.wait_recv()


def wide(u):
    return pl.ds(u * HALF, HALF)


def full(ref, u, s):
    return ref.at[:, s, :, wide(u)]


def half(ref, u, s, e):
    return ref.at[e, s, :, wide(u)]


class Gather:
    def __init__(self, net, ref, xp, yu, yd):
        self.net, self.ref, self.xp, self.yu, self.yd = net, ref, xp, yu, yd

    def move(self, u, src, dst, to):
        return self.net.go(full(self.ref, u, src), full(self.ref, u, dst), to)

    def pass_on(self, u, src, dst, e, to):
        return self.net.go(half(self.ref, u, src, e), half(self.ref, u, dst, e), to)

    def start0(self):
        self.x0 = self.move(0, 0, 4, self.xp)
        self.u00 = self.move(0, 0, 3, self.yu)
        self.d00 = self.move(0, 0, 1, self.yd)

    def start1(self):
        self.u1 = self.move(1, 0, 3, self.yu)
        self.d1 = self.move(1, 0, 1, self.yd)
        self.x1 = [self.move(1, 0, 4, self.xp)]

    def step2a(self):
        got(self.x0)
        self.u01 = self.move(0, 4, 7, self.yu)
        self.d01 = self.move(0, 4, 5, self.yd)

    def step2b(self):
        got(self.u1)
        self.fu1 = self.pass_on(1, 3, 2, 0, self.yu)
        self.x1.append(self.move(1, 3, 7, self.xp))
        got(self.d1)
        self.fd1 = self.pass_on(1, 1, 2, 1, self.yd)
        self.x1.append(self.move(1, 1, 5, self.xp))
        got(self.u00)
        self.fu00 = self.pass_on(0, 3, 2, 0, self.yu)
        got(self.d00)
        self.fd00 = self.pass_on(0, 1, 2, 1, self.yd)

    def step3(self):
        got(self.fu1, self.fd1)
        self.x1.append(self.move(1, 2, 6, self.xp))
        got(self.u01)
        self.fu01 = self.pass_on(0, 7, 6, 0, self.yu)
        got(self.d01)
        self.fd01 = self.pass_on(0, 5, 6, 1, self.yd)

    def finish(self):
        got(self.fu00, self.fd00, self.fu01, self.fd01)
        got(*self.x1)


class Reduce:
    def __init__(self, net, part, near, far, across, xp, yu, yd):
        self.net, self.p, self.near, self.far, self.across = net, part, near, far, across
        self.xp, self.yu, self.yd = xp, yu, yd
        self.ring = {}

    def outer(self, key, u, b):
        self.ring[key] = [
            self.net.go(half(self.p, u, b + 2, 0), self.near.at[key, 0], self.yu),
            self.net.go(half(self.p, u, b + 2, 1), self.near.at[key, 1], self.yd),
        ]

    def free_up(self, key, u, b):
        self.ring[key].append(self.net.go(half(self.p, u, b + 1, 1), self.far.at[key, 0, 1], self.yu))

    def free_down(self, key, u, b):
        self.ring[key].append(self.net.go(half(self.p, u, b + 3, 0), self.far.at[key, 1, 0], self.yd))

    def add(self, e, s, u, arrived):
        cols = wide(u)
        self.p[e, s, :, cols] = (self.p[e, s, :, cols].astype(F32) + arrived.astype(F32)).astype(BF)

    def inner(self, key, u, b):
        got(self.ring[key][0])
        self.add(0, b + 1, u, self.near[key, 0])
        up = self.net.go(half(self.p, u, b + 1, 0), self.far.at[key, 0, 0], self.yu)
        got(self.ring[key][1])
        self.add(1, b + 3, u, self.near[key, 1])
        down = self.net.go(half(self.p, u, b + 3, 1), self.far.at[key, 1, 1], self.yd)
        self.ring[key] += [up, down]

    def total(self, key, u, b):
        got(*self.ring[key][2:])
        return self.p[:, b, :, wide(u)].astype(F32) + self.far[key, 0].astype(F32) + self.far[key, 1].astype(F32)

    def start0(self):
        for dx in (1, 0):
            self.outer(dx, 0, 4 * dx)
        for dx in (1, 0):
            self.free_up(dx, 0, 4 * dx)
            self.free_down(dx, 0, 4 * dx)

    def start1(self):
        self.x1 = {dy: self.net.go(full(self.p, 1, 4 + dy), self.across.at[dy], self.xp) for dy in (2, 1, 3, 0)}

    def joined(self, dy):
        got(self.x1[dy])
        for e in range(EXP):
            self.add(e, dy, 1, self.across[dy, e])

    def step_a(self):
        self.joined(2)
        self.outer(2, 1, 0)
        self.inner(1, 0, 4)

    def step_b(self):
        self.inner(0, 0, 0)
        self.joined(1)
        self.free_up(2, 1, 0)

    def step_c(self):
        self.p[:, 4, :, wide(0)] = self.total(1, 0, 4).astype(BF)
        self.x0 = self.net.go(full(self.p, 0, 4), self.across.at[4], self.xp)

    def step_d(self):
        self.joined(3)
        self.free_down(2, 1, 0)
        self.inner(2, 1, 0)

    def final0(self):
        rows = self.total(0, 0, 0)
        got(self.x0)
        return (rows + self.across[4].astype(F32)).astype(BF).reshape(EXP * ROWS, HALF)

    def final1(self):
        self.joined(0)
        return self.total(2, 1, 0).astype(BF).reshape(EXP * ROWS, HALF)


def kernel(
    ids, gw, tok_in, cot_in, wg, wu, wd,
    pick_out, arr_o, arr_v, sum_d, sum_gu, far_d, far_gu,
    send_x, send_d, send_o, send_v, arr_x, arr_d, via,
    xg, dg, po, pv, near_o, far_o, across_o, near_v, far_v, across_v,
    tok, cot, pick, wgu, wdn, fac_a, fac_b, hid, dgu, pd, pgu, rd, rgu,
    send, recv, local,
):
    dp, z = lax.axis_index("dp"), lax.axis_index("expert")
    core, x, y = dp % 2, (dp // 2) % 4, dp // 8

    def at(yy, xx, cc):
        return ((yy * 4 + xx) * 2 + cc, z)

    xp = at(y, x + 1 - 2 * (x % 2), core)
    xc = at(y, 3 - x, core)
    yu, yd = at((y + 1) % 4, x, core), at((y + 3) % 4, x, core)
    cp = at(y, x, 1 - core)
    zs = {r: (dp, (z + r) % 4) for r in (1, 2, 3)}

    barrier = pltpu.get_barrier_semaphore()
    for device in (xp, xc, yu, yd, cp, zs[1], zs[2], zs[3]):
        pl.semaphore_signal(barrier, inc=1, device_id=device, device_id_type=MESH)

    tokens_in = [pltpu.make_async_copy(tok_in, tok, local.at[13]), pltpu.make_async_copy(cot_in, cot, local.at[14])]
    own = [
        pltpu.make_async_copy(wg, wgu.at[:, :, pl.ds(0, FP)], local.at[0]),
        pltpu.make_async_copy(wu, wgu.at[:, :, pl.ds(HID, FP)], local.at[1]),
        pltpu.make_async_copy(wd, wdn.at[:, pl.ds(0, FP), :], local.at[2]),
    ]
    for copy in tokens_in + own:
        copy.start()

    expert = lax.broadcasted_iota(jnp.int32, (2 * PLANES, TOK), 0)
    hot = [jnp.where(expert == ids[k : k + 1, :], 1.0, 0.0) for k in range(2)]
    row_t = lax.broadcasted_iota(jnp.int32, (TOK, TOK), 0)
    col_t = lax.broadcasted_iota(jnp.int32, (TOK, TOK), 1)
    before = dot((hot[0] + hot[1]).astype(BF), jnp.where(row_t < col_t, 1.0, 0.0).astype(BF))
    slab_row = lax.broadcasted_iota(jnp.int32, (ALL, TOK), 0).astype(F32)
    picks = []
    for k in range(2):
        e = ids[k : k + 1, :]
        plane = lax.shift_right_logical(e, 1)
        rel = plane - z
        rel = jnp.where(rel < 0, rel + PLANES, rel)
        base = rel * SLAB + (e - 2 * plane) * CAP
        place = jnp.sum(hot[k] * before, axis=0, keepdims=True)
        picks.append(jnp.where(slab_row == base.astype(F32) + place, 1.0, 0.0).astype(BF))
        pick[k] = picks[k]

    net = Net(send, recv)
    go = net.go

    class Exchange:
        def __init__(self, send_ref, arr_ref, via_ref, keep=None):
            self.send, self.arr, self.via, self.keep = send_ref, arr_ref, via_ref, keep
            self.first, self.copies, self.own = {}, {}, []

        def fill(self, rows, *units):
            for r in range(PLANES):
                part = rows[r * SLAB : (r + 1) * SLAB].astype(BF)
                ref = self.arr if r == 0 and self.keep is None else self.send
                if len(units) == 2:
                    ref[r] = part
                else:
                    ref[r, :, wide(units[0])] = part

        def start(self, u):
            lo, hi = pl.ds(u * HALF, HALF // 2), pl.ds(u * HALF + HALF // 2, HALF // 2)
            self.first[u] = go(self.send.at[2, :, hi], self.via.at[u], zs[3])
            self.copies[u] = [go(self.send.at[2, :, lo], self.arr.at[2, :, lo], zs[2])]
            self.copies[u] += [go(self.send.at[r, :, wide(u)], self.arr.at[PLANES - r, :, wide(u)], zs[r]) for r in (3, 1)]
            if self.keep is not None:
                own = pltpu.make_async_copy(self.send.at[0, :, wide(u)], self.arr.at[0, :, wide(u)], self.keep.at[u])
                own.start()
                self.own.append(own)

        def forward(self, u):
            got(self.first[u])
            hi = pl.ds(u * HALF + HALF // 2, HALF // 2)
            self.copies[u].append(go(self.via.at[u], self.arr.at[2, :, hi], zs[3]))

        def finish(self, u):
            got(*self.copies[u])

    ex = Exchange(send_x, arr_x, via.at[0])
    tokens_in[0].wait()
    ex.fill(dot(picks[0] + picks[1], tok[...]), 0, 1)
    pl.semaphore_wait(barrier, 8)
    ex.start(0)
    ex.start(1)

    def weight(k, lo):
        return wgu.at[:, :, pl.ds(lo + k * FP, FP)]

    def down(k):
        return wdn.at[:, pl.ds(k * FP, FP), :]

    cross = [go(wg, weight(1, 0), xc), go(wu, weight(1, HID), xc), go(wd, down(1), xc)]
    side = [go(wg, weight(2, 0), cp), go(wu, weight(2, HID), cp), go(wd, down(2), cp)]

    tokens_in[1].wait()
    cotf = cot[...].astype(F32)
    rows_d = [(jnp.sum(jnp.where(row_t == col_t, gw[k : k + 1, :], 0.0), axis=1, keepdims=True) * cotf).astype(BF) for k in range(2)]
    ed = Exchange(send_d, arr_d, via.at[1])
    ed.fill(dot(picks[0], rows_d[0]) + dot(picks[1], rows_d[1]), 0, 1)

    def from_slab(c):
        s = (c >= SLAB).astype(jnp.int32) + (c >= 2 * SLAB).astype(jnp.int32) + (c >= 3 * SLAB).astype(jnp.int32)
        rest = c - SLAB * s
        j = (rest >= CAP).astype(jnp.int32)
        row = j * ROWS + s * CAP + rest - CAP * j
        return jnp.where(rest < EXP * CAP, row, -1)

    into = jnp.where(
        from_slab(lax.broadcasted_iota(jnp.int32, (EXP * ROWS, ALL), 1))
        == lax.broadcasted_iota(jnp.int32, (EXP * ROWS, ALL), 0), 1.0, 0.0,
    ).astype(BF)
    back = jnp.where(
        from_slab(lax.broadcasted_iota(jnp.int32, (ALL, EXP * ROWS), 0))
        == lax.broadcasted_iota(jnp.int32, (ALL, EXP * ROWS), 1), 1.0, 0.0,
    ).astype(BF)

    def chunk_in(arr_ref, g, u):
        rows = dot(into, arr_ref[:, :, wide(u)].reshape(ALL, HALF)).astype(BF)
        g[0, 0, :, wide(u)] = rows[:ROWS]
        g[1, 0, :, wide(u)] = rows[ROWS:]

    gx, gd = Gather(net, xg, xp, yu, yd), Gather(net, dg, xp, yu, yd)
    ex.forward(0)
    ex.finish(0)
    chunk_in(arr_x, xg, 0)
    gx.start0()
    ex.forward(1)
    ex.finish(1)
    chunk_in(arr_x, xg, 1)
    gx.start1()
    ed.start(0)
    ed.start(1)
    gx.step2a()
    ed.forward(0)
    ed.forward(1)
    gx.step2b()
    ed.finish(0)
    ed.finish(1)
    chunk_in(arr_d, dg, 0)
    chunk_in(arr_d, dg, 1)
    gd.start0()
    gd.start1()
    got(cross[0])
    side.append(go(weight(1, 0), weight(3, 0), cp))
    gx.step3()
    got(cross[1])
    side.append(go(weight(1, HID), weight(3, HID), cp))
    for copy in own:
        copy.wait()
    got(*side)

    def forward(e):
        def tile(n, _):
            cols = pl.ds(pl.multiple_of(n * 256, 256), 256)
            rows = xg[e].reshape(MINE, D)
            gate = dot(rows, wgu[e, :, cols])
            up = dot(rows, wgu[e, :, pl.ds(pl.multiple_of(n * 256 + HID, 256), 256)])
            sig = 1.0 / (1.0 + jnp.exp(-gate))
            act = gate * sig
            hid[e, :, cols] = (act * up).astype(BF)
            fac_b[e, :, cols] = act
            fac_a[e, :, cols] = up * sig * (1.0 + gate * (1.0 - sig))
            return 0

        lax.fori_loop(0, HID // 256, tile, 0)

    def project(u):
        def tile(i, _):
            e, cols = i // 2, pl.ds(pl.multiple_of(u * HALF + (i % 2) * 256, 256), 256)
            po[e, :, :, cols] = dot(hid[e], wdn[e, :, cols]).astype(BF).reshape(SLOTS, ROWS, 256)
            return 0

        lax.fori_loop(0, 2 * EXP, tile, 0)

    gx.finish()
    forward(0)
    gd.step2a()
    gd.step2b()
    forward(1)
    gd.step3()
    got(cross[2])
    late = go(down(1), down(3), cp)
    got(late)
    ro = Reduce(net, po, near_o, far_o, across_o, xp, yu, yd)
    rv = Reduce(net, pv, near_v, far_v, across_v, xp, yu, yd)
    project(1)
    ro.start1()
    project(0)
    ro.start0()

    def backward(e):
        def tile(n, _):
            cols = pl.ds(pl.multiple_of(n * 256, 256), 256)
            dact = dot(dg[e].reshape(MINE, D), wdn[e, cols, :], (1, 1))
            dgu[e, :, cols] = (dact * fac_a[e, :, cols]).astype(BF)
            dgu[e, :, pl.ds(pl.multiple_of(n * 256 + HID, 256), 256)] = (dact * fac_b[e, :, cols]).astype(BF)
            return 0

        lax.fori_loop(0, HID // 256, tile, 0)

    def propagate(u):
        def tile(i, _):
            e, cols = i // 2, pl.ds(pl.multiple_of(u * HALF + (i % 2) * 256, 256), 256)
            part = dot(dgu[e], wgu[e, cols, :], (1, 1))
            pv[e, :, :, cols] = part.astype(BF).reshape(SLOTS, ROWS, 256)
            return 0

        lax.fori_loop(0, 2 * EXP, tile, 0)

    def down_grad(e):
        def tile(n, _):
            cols = pl.ds(pl.multiple_of(n * 256, 256), 256)
            pd[e, cols, :] = dot(hid[e, :, cols], dg[e].reshape(MINE, D), (0, 0)).astype(BF)
            return 0

        lax.fori_loop(0, HID // 256, tile, 0)

    def up_grad(e):
        def tile(n, _):
            cols = pl.ds(pl.multiple_of(n * 256, 256), 256)
            pgu[e, cols, :] = dot(xg[e, :, :, cols].reshape(MINE, 256), dgu[e], (0, 0)).astype(BF)
            return 0

        lax.fori_loop(0, D // 256, tile, 0)

    pair = 2 * FP
    share, kept = {}, []

    def keep(src, dst):
        copy = pltpu.make_async_copy(src, dst, local.at[3 + len(kept)])
        copy.start()
        kept.append(copy)

    def share_down(e):
        share["d", e] = go(pd.at[e, pl.ds(pair, pair), :], rd.at[e], cp)

    def share_up(e):
        for i in range(2):
            share[i, e] = go(pgu.at[e, :, pl.ds(i * HID + pair, pair)], rgu.at[i, e], cp)

    far = []

    def send_down(e):
        got(share["d", e])
        pd[e, pl.ds(0, pair), :] = (pd[e, pl.ds(0, pair), :].astype(F32) + rd[e].astype(F32)).astype(BF)
        far.append(go(pd.at[e, pl.ds(FP, FP), :], far_d.at[e], xc))
        keep(pd.at[e, pl.ds(0, FP), :], sum_d.at[e])

    def send_up(e):
        for i in range(2):
            got(share[i, e])
            cols = pl.ds(i * HID, pair)
            pgu[e, :, cols] = (pgu[e, :, cols].astype(F32) + rgu[i, e].astype(F32)).astype(BF)
            far.append(go(pgu.at[e, :, pl.ds(i * HID + FP, FP)], far_gu.at[i, e], xc))
            keep(pgu.at[e, :, pl.ds(i * HID, FP)], sum_gu.at[i, e])

    picks_out = pltpu.make_async_copy(pick, pick_out, local.at[15])
    picks_out.start()
    gd.finish()
    down_grad(0)
    share_down(0)
    backward(0)
    ro.step_a()
    down_grad(1)
    share_down(1)
    send_down(0)
    backward(1)
    send_down(1)
    ro.step_b()
    up_grad(0)
    share_up(0)
    ro.step_c()
    propagate(1)
    rv.start1()
    ro.step_d()
    send_up(0)
    propagate(0)
    rv.start0()
    eo = Exchange(send_o, arr_o, via.at[2], local.at[pl.ds(9, 2)])
    ev = Exchange(send_v, arr_v, via.at[3], local.at[pl.ds(11, 2)])
    up_grad(1)
    share_up(1)
    eo.fill(dot(back, ro.final1()), 1)
    eo.start(1)
    eo.fill(dot(back, ro.final0()), 0)
    eo.start(0)
    send_up(1)
    rv.step_a()
    eo.forward(1)
    eo.forward(0)
    rv.step_b()
    rv.step_d()
    rv.step_c()
    ev.fill(dot(back, rv.final1()), 1)
    ev.start(1)
    ev.fill(dot(back, rv.final0()), 0)
    ev.start(0)
    ev.forward(1)
    ev.forward(0)
    for u in range(2):
        eo.finish(u)
        ev.finish(u)
    got(*far)
    for copy in kept + eo.own + ev.own + [picks_out]:
        copy.wait()
    for copy in net.all:
        copy.wait_send()


def finish(gw, pick, arr_o, arr_v, sum_d, sum_gu, far_d, far_gu, mixed, gtok, ggate, gup, gdown):
    eye = lax.broadcasted_iota(jnp.int32, (TOK, TOK), 0) == lax.broadcasted_iota(jnp.int32, (TOK, TOK), 1)
    rows = arr_o[...].reshape(ALL, D)
    total = jnp.zeros((TOK, D), F32)
    for k in range(2):
        weight = jnp.sum(jnp.where(eye, gw[k : k + 1, :], 0.0), axis=1, keepdims=True)
        total = total + weight * dot(pick[k], rows, (0, 0))
    mixed[...] = total.astype(BF)
    gtok[...] = dot(pick[0] + pick[1], arr_v[...].reshape(ALL, D), (0, 0)).astype(BF)
    gdown[...] = (sum_d[...].astype(F32) + far_d[...].astype(F32)).astype(BF)
    ggate[...] = (sum_gu[0].astype(F32) + far_gu[0].astype(F32)).astype(BF)
    gup[...] = (sum_gu[1].astype(F32) + far_gu[1].astype(F32)).astype(BF)


def body(tokens, expert_ids, gate_weights, w_gate, w_up, w_down, cotangent):
    vmem, hbm = pl.BlockSpec(memory_space=pltpu.VMEM), pl.BlockSpec(memory_space=pl.ANY)

    def buf(*shape, dtype=BF):
        return pltpu.VMEM(shape, dtype)

    slab = [buf(PLANES, SLAB, D) for _ in range(6)]
    big = [buf(EXP, SLOTS, ROWS, D) for _ in range(4)]
    rings = [buf(3, 2, ROWS, HALF), buf(3, 2, EXP, ROWS, HALF), buf(5, EXP, ROWS, HALF)] * 2
    scratch = slab + [buf(4, 2, SLAB, HALF // 2)] + big + rings + [
        buf(TOK, D), buf(TOK, D), buf(2, ALL, TOK),
        buf(EXP, D, 2 * HID), buf(EXP, HID, D),
        buf(EXP, MINE, HID, dtype=F32), buf(EXP, MINE, HID, dtype=F32),
        buf(EXP, MINE, HID), buf(EXP, MINE, 2 * HID),
        buf(EXP, HID, D), buf(EXP, D, 2 * HID),
        buf(EXP, 2 * FP, D), buf(2, EXP, D, 2 * FP),
        pltpu.SemaphoreType.DMA((COPIES,)), pltpu.SemaphoreType.DMA((COPIES,)), pltpu.SemaphoreType.DMA((16,)),
    ]

    def out(*shape):
        return jax.ShapeDtypeStruct(shape, BF)

    weights = gate_weights.T
    parts = pl.pallas_call(
        kernel,
        out_shape=(
            out(2, ALL, TOK), out(PLANES, SLAB, D), out(PLANES, SLAB, D),
            out(EXP, FP, D), out(2, EXP, D, FP), out(EXP, FP, D), out(2, EXP, D, FP),
        ),
        in_specs=[vmem] * 2 + [hbm] * 5,
        out_specs=(hbm,) * 7,
        scratch_shapes=scratch,
        compiler_params=pltpu.CompilerParams(
            collective_id=0, has_side_effects=True, vmem_limit_bytes=67043328
        ),
    )(expert_ids.T, weights, tokens, cotangent, w_gate, w_up, w_down)
    return pl.pallas_call(
        finish,
        out_shape=tuple(
            jax.ShapeDtypeStruct(a.shape, BF) for a in (tokens, tokens, w_gate, w_up, w_down)
        ),
        in_specs=[vmem] * 8,
        out_specs=(vmem,) * 5,
    )(weights, *parts)


def solution(mesh):
    rows = P(("dp", "expert"), None)
    cols = P("expert", None, "dp")
    down = P("expert", "dp", None)
    return jax.shard_map(
        body,
        mesh=mesh,
        in_specs=(rows, rows, rows, cols, cols, down, rows),
        out_specs=(rows, rows, cols, cols, down),
        check_vma=False,
    )
```
